32 devices in a mesh: parts: 2 (over x), owner: 16 (over z, y, core).
Axes of the slice: x: 2, y: 2, z: 4, core: 2. Of those that a mesh axis runs over, the one named last changes fastest.
Arguments:
- embeddings: bfloat16 [32768, 768], P(('parts', 'owner')), parts along dimension 0, may hold values from -6 to 6
- cluster_ids: int32 [32768], P(('parts', 'owner')), parts along dimension 0, may hold values from 0 to 63, as said below
- owner_map: int32 [128], P('parts'), parts along dimension 0, may hold values from 0 to 15, as said below
Outputs:
- maxima: float32 [32768], P(('parts', 'owner')), parts along dimension 0
- cluster_mean: float32 [128], P('parts'), parts along dimension 0
The draws below stay inside these ranges and needn't reach their ends.
There are 2 independent parts, one for each index of `parts`. The reference program is written for one: setup_inputs(seed, part) draws one part's arguments, and reference() takes and returns one part's arrays. A program takes and returns all parts, laid end to end along the dimension named above; each array names one. Nothing has to cross between parts.
Inputs may be any that keep to these rules, and one draw needn't show every extreme that they name: `cluster_ids`: cluster of each item. Owners 2k and 2k+1 form a pair; exactly 128 of the items of one device belong to clusters of one pair, so at most 128 to one owner, and in every draw some owner receives exactly 128 items from every device. `owner_map`: every owner owns exactly 4 clusters.
All inputs are finite; a program needn't handle non-finite values.
Results may differ from the reference program's by a relative error of at most 0.0015.
Values may be sent and summed in bfloat16 or wider, within the bound.
No kernel may reach another device: no remote copies, remote signals or barrier semaphores. Data moves between devices by JAX's collectives and lax.ppermute only.
A program may use at most 64 MiB of HBM per device.

```python
import jax
import jax.numpy as jnp
from jax import lax

D = 768
ITEMS_DEV = 1024
CL_DEV = 4
CAP = 128
ITEMS = 16384
CLUSTERS = 64
N_OWNER = 16


def route_tables(key):
    base = jax.random.fold_in(key, 7)
    key_perm, key_thresh, key_hot, key_flip, key_items = jax.random.split(base, 5)
    perm = jax.random.permutation(key_perm, CLUSTERS).astype(jnp.int32)
    owner_map = (perm // CL_DEV).astype(jnp.int32)
    inverse = jnp.argsort(perm).astype(jnp.int32)
    cluster_list = inverse.reshape(N_OWNER, CL_DEV)
    pair_count = N_OWNER // 2
    thresh = jax.random.randint(key_thresh, (pair_count,), 1, 8, dtype=jnp.int32)
    hottest = jax.random.randint(key_hot, (), 0, pair_count, dtype=jnp.int32)
    thresh = jnp.where(jnp.arange(pair_count, dtype=jnp.int32) == hottest, 8, thresh)
    flip = jax.random.randint(key_flip, (pair_count,), 0, 2, dtype=jnp.int32)

    def one_source(source_key):
        key_order, key_side, key_left, key_right = jax.random.split(source_key, 4)
        pair_of = jax.random.permutation(key_order, jnp.arange(ITEMS_DEV, dtype=jnp.int32) // CAP)
        side = (jax.random.randint(key_side, (ITEMS_DEV,), 0, 8, dtype=jnp.int32) < thresh[pair_of]).astype(jnp.int32)
        chosen = 2 * pair_of + jnp.abs(side - flip[pair_of])
        left = jax.random.randint(key_left, (ITEMS_DEV,), 0, CL_DEV, dtype=jnp.int32)
        right = jax.random.randint(key_right, (ITEMS_DEV,), 0, CL_DEV, dtype=jnp.int32)
        return cluster_list[chosen, jnp.minimum(left, right)]
    cluster_ids = jax.vmap(one_source)(jax.random.split(key_items, N_OWNER)).reshape(-1).astype(jnp.int32)
    return (owner_map, cluster_ids)


def draw_cluster_ids(key, part):
    return route_tables(key)[1]


def draw_owner_map(key, part):
    return route_tables(key)[0]


def steps_of(rng, shape, shards, low, high):
    factor_of, own = 1.0, jax.random.fold_in(rng, 6)
    for dim, shards_of in shards:
        steps = jnp.exp(jax.random.uniform(jax.random.fold_in(own, dim), (shards_of,), jnp.float32, low / len(shards), high / len(shards)))
        factor_of = factor_of * jnp.repeat(steps, shape[dim] // shards_of).reshape([-1 if axis == dim else 1 for axis in range(len(shape))])
    return factor_of


def normal_values(rng, shape, deviation, reach, pieces=(), held_as=jnp.bfloat16):
    gain = steps_of(rng, shape, pieces, -0.22, 0.18) if pieces else 1.0
    entries = jax.random.normal(rng, shape, jnp.float32) * deviation * gain
    return jnp.minimum(jnp.maximum(entries, -reach), reach).astype(held_as)


def setup_inputs(seed: int = 0, part: int = 0) -> dict:
    seeds = jax.random.split(jax.random.key(seed), 4)
    part_keys = jax.random.split(jax.random.fold_in(seeds[3], part), 4)
    embeddings = normal_values(part_keys[0], (ITEMS, D), 1.0, 6.0, ((0, 16),))
    cluster_ids = draw_cluster_ids(jax.random.fold_in(jax.random.fold_in(seeds[3], part), 71), part)
    owner_map = draw_owner_map(jax.random.fold_in(jax.random.fold_in(seeds[3], part), 71), part)
    return dict(embeddings=embeddings, cluster_ids=cluster_ids, owner_map=owner_map)


def unitize(rows):
    values = rows.astype(jnp.float32)
    scale = lax.rsqrt(lax.optimization_barrier(jnp.mean(values * values, axis=-1, keepdims=True)) + 1e-06)
    return (values * scale / jnp.sqrt(jnp.float32(D))).astype(jnp.bfloat16)

def reference(embeddings, cluster_ids, owner_map):
    total_items = ITEMS_DEV * N_OWNER
    received = N_OWNER * CAP
    unit = unitize(embeddings).astype(jnp.float32)
    owner_of = owner_map[cluster_ids]
    positions = jnp.arange(received, dtype=jnp.int32)
    distinct = positions[:, None] != positions[None, :]

    def per_owner(carry, owner):
        order = jnp.argsort((owner_of != owner).astype(jnp.int32), stable=True)[:received].astype(jnp.int32)
        valid = owner_of[order] == owner
        labels = jnp.where(valid, cluster_ids[order], -1)
        rows = unit[order]
        gram = jnp.dot(rows, rows.T, precision=lax.Precision.HIGHEST, preferred_element_type=jnp.float32)
        mask = (labels[:, None] == labels[None, :]) & (labels[:, None] >= 0) & distinct
        best = lax.optimization_barrier(jnp.max(jnp.where(mask, gram, jnp.float32(-1.0)), axis=1))
        target = jnp.where(valid, order, total_items).astype(jnp.int32)
        return (carry.at[target].set(best, mode='drop'), None)
    start = jnp.full((total_items,), -1.0, jnp.float32)
    maxima, _ = lax.scan(per_owner, start, jnp.arange(N_OWNER, dtype=jnp.int32))
    totals = jax.ops.segment_sum(maxima, cluster_ids, num_segments=CLUSTERS)
    counts = jax.ops.segment_sum(jnp.ones_like(maxima), cluster_ids, num_segments=CLUSTERS)
    return (maxima, totals / jnp.maximum(counts, 1.0))
```

```python
import functools

import jax
import jax.numpy as jnp
from jax import lax
from jax.experimental import pallas as pl
from jax.experimental.pallas import tpu as pltpu
from jax.sharding import PartitionSpec as P


LANES = 128
EXTRA = 16
F32 = jnp.float32
BF16 = jnp.bfloat16


def iota(shape, dim):
    return lax.broadcasted_iota(jnp.int32, shape, dim)


def lane_take(row, index):
    if index.shape[0] == 1:
        return lane_take(row, jnp.broadcast_to(index, (8, LANES)))[0:1, :]
    out = None
    for first in range(0, row.shape[1], LANES):
        piece = jnp.broadcast_to(row[:, first : first + LANES], index.shape)
        local = index - first
        inside = (local >= 0) & (local < LANES)
        taken = jnp.take_along_axis(
            piece, jnp.where(inside, local, 0), axis=1, mode="promise_in_bounds"
        )
        out = taken if out is None else jnp.where(inside, taken, out)
    return out


def send_kernel(ids_ref, owners_ref, rows_ref, *refs, pairs, capacity, clusters):
    blocks = refs[:pairs]
    pair_ref, rank_ref, table_ref, rows, row_pad, sem = refs[pairs:]
    copy = pltpu.make_async_copy(rows_ref, rows, sem)
    copy.start()
    chip = lax.axis_index("owner") // 2
    chunks = ids_ref.shape[0]
    padded = row_pad.shape[1]
    row_pad[...] = jnp.full(row_pad.shape, -2, jnp.int32)
    row_pad[0:1, 0:clusters] = owners_ref[...]
    pair_row = row_pad[0:1, :] >> 1
    across = jnp.broadcast_to(pair_row, (padded, padded))
    down = across.astype(F32).T.astype(jnp.int32)
    before = (across == down) & (iota(across.shape, 0) < iota(across.shape, 1))
    local_row = jnp.sum(before.astype(F32), axis=0, keepdims=True).astype(jnp.int32)
    table_ref[0:1, :] = pair_row
    table_ref[1:2, :] = local_row
    ids = ids_ref[...]
    pair = lane_take(pair_row, ids)
    label = lane_take(local_row, ids).astype(F32)
    hots = [pair == (chip ^ m) for m in range(pairs)]
    hot = jnp.concatenate([h.astype(F32) for h in hots], axis=0)
    upper = (iota((LANES, LANES), 0) <= iota((LANES, LANES), 1)).astype(BF16)
    within = jnp.dot(hot.astype(BF16), upper, preferred_element_type=F32)
    sums = jnp.dot(hot.astype(BF16), jnp.ones((LANES, LANES), BF16), preferred_element_type=F32)
    r, c = iota((pairs * chunks,) * 2, 0), iota((pairs * chunks,) * 2, 1)
    earlier = ((r // chunks == c // chunks) & (c < r)).astype(BF16)
    offset = jnp.dot(earlier, sums.astype(BF16), preferred_element_type=F32)
    rank = jnp.where(hot > 0.0, within + offset - 1.0, -1.0)
    item_rank = rank[0:chunks, :]
    for m in range(1, pairs):
        item_rank = jnp.maximum(item_rank, rank[m * chunks : (m + 1) * chunks, :])
    pair_ref[...] = pair
    rank_ref[...] = item_rank.astype(jnp.int32)
    label_pad = jnp.concatenate(
        [label[k : k + 1, :] for k in range(chunks)], axis=1
    )
    label_pad = jnp.broadcast_to(label_pad, (16, chunks * LANES)).astype(BF16)
    width = rows.shape[1]
    place = iota((capacity, LANES), 0).astype(F32)
    copy.wait()
    for m in range(pairs):
        chosen = jnp.concatenate(
            [
                (place == rank[m * chunks + k : m * chunks + k + 1, :]).astype(F32).astype(BF16)
                for k in range(chunks)
            ],
            axis=1,
        )
        values = jnp.dot(chosen, rows[...], preferred_element_type=F32)
        scale = lax.rsqrt(jnp.mean(values * values, axis=1, keepdims=True) + 1e-06)
        unit = (values * scale * (1.0 / jnp.sqrt(F32(width)))).astype(BF16)
        labels = lax.dot_general(
            label_pad, chosen, (((1,), (1,)), ((), ())), preferred_element_type=F32
        )
        slabs = width // LANES
        for k in range(slabs):
            blocks[m][k * capacity : (k + 1) * capacity, :] = unit[:, k * LANES : (k + 1) * LANES]
        blocks[m][slabs * capacity : slabs * capacity + EXTRA, 0:capacity] = labels.astype(BF16)


def send_blocks(ids, owners, rows, pairs, capacity):
    clusters = owners.shape[1]
    padded = -(-clusters // LANES) * LANES
    width = rows.shape[1]
    height = width // LANES * capacity + EXTRA
    vmem = pl.BlockSpec(memory_space=pltpu.VMEM)
    return pl.pallas_call(
        functools.partial(send_kernel, pairs=pairs, capacity=capacity, clusters=clusters),
        in_specs=[vmem, vmem, pl.BlockSpec(memory_space=pl.ANY)],
        out_specs=[vmem] * (pairs + 3),
        out_shape=[jax.ShapeDtypeStruct((height, LANES), BF16)] * pairs
        + [jax.ShapeDtypeStruct(ids.shape, jnp.int32)] * 2
        + [jax.ShapeDtypeStruct((8, padded), jnp.int32)],
        scratch_shapes=[
            pltpu.VMEM(rows.shape, BF16),
            pltpu.VMEM((8, padded), jnp.int32),
            pltpu.SemaphoreType.DMA(()),
        ],
        name="send",
    )(ids, owners, rows)


def gram_kernel(*refs, pairs, capacity, labels_per_pair):
    own, other = refs[:pairs], refs[pairs : 2 * pairs]
    out_ref, keys, marks = refs[2 * pairs :]
    owner = lax.axis_index("owner")
    chip, core = owner // 2, owner % 2
    width = keys.shape[1]
    slabs = width // LANES
    items = pairs * capacity
    for b, block in enumerate(own + other):
        at = b * capacity
        for k in range(slabs):
            keys[at : at + capacity, k * LANES : (k + 1) * LANES] = block[
                k * capacity : (k + 1) * capacity, :
            ]
        marks[0:1, at : at + capacity] = block[
            slabs * capacity : slabs * capacity + EXTRA, 0:capacity
        ].astype(F32)[0:1, :]
    query_marks = marks[0:1, 0:items]
    best = [jnp.full((8, LANES), -1.0, F32) for _ in range(0, items, LANES)]
    step = 2 * LANES
    for first in range(0, 2 * items, step):
        gram = lax.dot_general(
            keys[first : first + step, :],
            keys[0:items, :],
            (((1,), (1,)), ((), ())),
            preferred_element_type=F32,
        )
        for half in range(0, step, LANES):
            at = first + half
            column = jnp.broadcast_to(marks[0:1, at : at + LANES], (LANES, LANES)).T
            for tile in range(0, items, LANES):
                same = column == query_marks[:, tile : tile + LANES]
                if tile == at:
                    same = same & (iota((LANES, LANES), 0) != iota((LANES, LANES), 1))
                piece = jnp.where(same, gram[half : half + LANES, tile : tile + LANES], -1.0)
                top = jnp.max(piece.reshape(LANES // 8, 8, LANES), axis=0)
                best[tile // LANES] = jnp.maximum(best[tile // LANES], top)
    row = jnp.concatenate([jnp.max(b, axis=0, keepdims=True) for b in best], axis=1)
    lane = iota((1, LANES), 1)
    stats = jnp.zeros((1, LANES), F32)
    for k in range(labels_per_pair):
        mine = query_marks == k
        total = jnp.sum(jnp.where(mine, row, 0.0), axis=1, keepdims=True)
        number = jnp.sum(mine.astype(F32), axis=1, keepdims=True)
        stats = jnp.where(lane == k, total, stats)
        stats = jnp.where(lane == labels_per_pair + k, number, stats)
    for d in range(2 * pairs):
        out_ref[d, 1:2, :] = stats
    marks[1:2, 0:items] = row
    for m in range(pairs):
        out_ref[2 * (chip ^ m) + core, 0:1, 0:capacity] = marks[
            1:2, m * capacity : (m + 1) * capacity
        ]


def gram_best(own, other, width, capacity, labels_per_pair):
    pairs = len(own)
    items = pairs * capacity
    vmem = pl.BlockSpec(memory_space=pltpu.VMEM)
    return pl.pallas_call(
        functools.partial(
            gram_kernel, pairs=pairs, capacity=capacity, labels_per_pair=labels_per_pair
        ),
        in_specs=[vmem] * (2 * pairs),
        out_specs=vmem,
        out_shape=jax.ShapeDtypeStruct((2 * pairs, 8, LANES), F32),
        scratch_shapes=[
            pltpu.VMEM((2 * items, width), BF16),
            pltpu.VMEM((8, 2 * items), F32),
        ],
        name="gram",
    )(*own, *other)


def finish_kernel(back_ref, pair_ref, rank_ref, table_ref, maxima_ref, mean_ref, *, pairs, labels_per_pair):
    core = lax.axis_index("owner") % 2
    pair, rank = pair_ref[...], rank_ref[...]
    maxima = jnp.zeros(pair.shape, F32)
    padded = table_ref.shape[1]
    pair_row, local_row = table_ref[0:1, :], table_ref[1:2, :]
    total = jnp.zeros((1, padded), F32)
    number = jnp.zeros((1, padded), F32)
    for p in range(pairs):
        got = lane_take(back_ref[2 * p + core, 0:1, :], rank)
        maxima = jnp.where(pair == p, got, maxima)
        stats = back_ref[2 * p, 1:2, :] + back_ref[2 * p + 1, 1:2, :]
        mine = pair_row == p
        index = jnp.where(mine, local_row, 0)
        parts = [index[:, f : f + LANES] for f in range(0, padded, LANES)]
        sums = jnp.concatenate([lane_take(stats, i) for i in parts], axis=1)
        counts = jnp.concatenate([lane_take(stats, i + labels_per_pair) for i in parts], axis=1)
        total = jnp.where(mine, sums, total)
        number = jnp.where(mine, counts, number)
    maxima_ref[...] = maxima
    mean = total / jnp.maximum(number, 1.0)
    mean_ref[...] = mean[:, : mean_ref.shape[1]]


def finish(back, pair, rank, table, clusters, pairs, labels_per_pair):
    vmem = pl.BlockSpec(memory_space=pltpu.VMEM)
    return pl.pallas_call(
        functools.partial(finish_kernel, pairs=pairs, labels_per_pair=labels_per_pair),
        in_specs=[vmem] * 4,
        out_specs=[vmem] * 2,
        out_shape=[
            jax.ShapeDtypeStruct(pair.shape, F32),
            jax.ShapeDtypeStruct((1, clusters), F32),
        ],
        name="finish",
    )(back, pair, rank, table)


def body(embeddings, cluster_ids, owner_map):
    owners = lax.axis_size("owner")
    items, width = embeddings.shape
    clusters = owner_map.shape[0]
    pairs = owners // 2
    capacity = items // pairs
    labels_per_pair = clusters // pairs
    ids = cluster_ids.reshape(items // LANES, LANES)
    *blocks, pair, rank, table = send_blocks(
        ids, owner_map.reshape(1, clusters), embeddings, pairs, capacity
    )
    swap = [(d, d ^ 1) for d in range(owners)]
    own, other = [], []
    for m in range(pairs):
        block = blocks[m]
        if m:
            block = lax.ppermute(block, "owner", [(d, d ^ (2 * m)) for d in range(owners)])
        own.append(block)
        other.append(lax.ppermute(block, "owner", swap))
    best = gram_best(own, other, width, capacity, labels_per_pair)
    back = lax.all_to_all(best, "owner", split_axis=0, concat_axis=0, tiled=True)
    maxima, mean = finish(back, pair, rank, table, clusters, pairs, labels_per_pair)
    return maxima.reshape(items), mean.reshape(clusters)


def solution(mesh):
    placed = (P(("parts", "owner"), None), P(("parts", "owner")), P("parts"))
    return jax.shard_map(
        body,
        mesh=mesh,
        in_specs=placed,
        out_specs=(P(("parts", "owner")), P("parts")),
        check_vma=False,
    )
```

```python
import functools

import jax
import jax.numpy as jnp
from jax import lax
from jax.experimental import pallas as pl
from jax.experimental.pallas import tpu as pltpu
from jax.sharding import PartitionSpec as P


LANES = 128
EXTRA = 16
F32 = jnp.float32
BF16 = jnp.bfloat16
VMEM = pl.BlockSpec(memory_space=pltpu.VMEM)
HBM = pl.BlockSpec(memory_space=pltpu.HBM)
PARAMS = pltpu.CompilerParams(vmem_limit_bytes=16 * 2**20)


def iota(shape, dim):
    return lax.broadcasted_iota(jnp.int32, shape, dim)


def near(value):
    return pltpu.with_memory_space_constraint(value, pltpu.VMEM)


def far(value):
    return pltpu.with_memory_space_constraint(value, pltpu.HBM)


def lane_take(row, index):
    if index.shape[0] == 1:
        return lane_take(row, jnp.broadcast_to(index, (8, LANES)))[0:1, :]
    out = None
    for first in range(0, row.shape[1], LANES):
        piece = jnp.broadcast_to(row[:, first : first + LANES], index.shape)
        local = index - first
        inside = (local >= 0) & (local < LANES)
        taken = jnp.take_along_axis(
            piece, jnp.where(inside, local, 0), axis=1, mode="promise_in_bounds"
        )
        out = taken if out is None else jnp.where(inside, taken, out)
    return out


def route(ids_ref, owners_ref, pair_ref, rank_ref, label_ref, table_ref, slot_ref, pad, pairs, clusters):
    chip = lax.axis_index("owner") // 2
    chunks = ids_ref.shape[0]
    padded = pad.shape[1]
    pad[...] = jnp.full(pad.shape, -2, jnp.int32)
    pad[0:1, 0:clusters] = owners_ref[...]
    pair_row = pad[0:1, :] >> 1
    across = jnp.broadcast_to(pair_row, (padded, padded))
    down = across.astype(F32).T.astype(jnp.int32)
    before = (across == down) & (iota(across.shape, 0) < iota(across.shape, 1))
    local_row = jnp.sum(before.astype(F32), axis=0, keepdims=True).astype(jnp.int32)
    table_ref[0:1, :] = pair_row
    table_ref[1:2, :] = local_row
    ids = ids_ref[...]
    pair = lane_take(pair_row, ids)
    label_ref[...] = lane_take(local_row, ids).astype(F32)
    hots = [pair == (chip ^ m) for m in range(pairs)]
    hot = jnp.concatenate([h.astype(F32) for h in hots], axis=0)
    upper = (iota((LANES, LANES), 0) <= iota((LANES, LANES), 1)).astype(BF16)
    within = jnp.dot(hot.astype(BF16), upper, preferred_element_type=F32)
    sums = jnp.dot(hot.astype(BF16), jnp.ones((LANES, LANES), BF16), preferred_element_type=F32)
    r, c = iota((pairs * chunks,) * 2, 0), iota((pairs * chunks,) * 2, 1)
    earlier = ((r // chunks == c // chunks) & (c < r)).astype(BF16)
    offset = jnp.dot(earlier, sums.astype(BF16), preferred_element_type=F32)
    slot = jnp.where(hot > 0.0, within + offset - 1.0, -1.0)
    item_rank = slot[0:chunks, :]
    for m in range(1, pairs):
        item_rank = jnp.maximum(item_rank, slot[m * chunks : (m + 1) * chunks, :])
    slot_ref[...] = slot
    pair_ref[...] = pair
    rank_ref[...] = item_rank.astype(jnp.int32)


def pack(slot_ref, label_ref, rows, blocks, numbers, capacity):
    chunks = label_ref.shape[0]
    width = rows.shape[1]
    slabs = width // LANES
    label = jnp.concatenate([label_ref[k : k + 1, :] for k in range(chunks)], axis=1)
    label = jnp.broadcast_to(label, (EXTRA, chunks * LANES)).astype(BF16)
    place = iota((capacity, LANES), 0).astype(F32)
    for block, m in zip(blocks, numbers):
        chosen = jnp.concatenate(
            [
                (place == slot_ref[m * chunks + k : m * chunks + k + 1, :]).astype(F32).astype(BF16)
                for k in range(chunks)
            ],
            axis=1,
        )
        values = jnp.dot(chosen, rows[...], preferred_element_type=F32)
        scale = lax.rsqrt(jnp.mean(values * values, axis=1, keepdims=True) + 1e-06)
        unit = (values * scale * (1.0 / jnp.sqrt(F32(width)))).astype(BF16)
        labels = lax.dot_general(
            label, chosen, (((1,), (1,)), ((), ())), preferred_element_type=F32
        )
        for k in range(slabs):
            block[k * capacity : (k + 1) * capacity, :] = unit[:, k * LANES : (k + 1) * LANES]
        block[slabs * capacity : slabs * capacity + EXTRA, 0:capacity] = labels.astype(BF16)


def first_kernel(ids_hbm, owners_hbm, rows_hbm, *refs, numbers, pairs, capacity, clusters):
    n = len(numbers)
    blocks = refs[:n]
    pair_ref, rank_ref, label_ref, table_ref, slot_ref, rows, ids_ref, owners_ref, pad, sems = refs[n:]
    copies = [
        pltpu.make_async_copy(source, target, sems.at[k])
        for k, (source, target) in enumerate(
            ((ids_hbm, ids_ref), (owners_hbm, owners_ref), (rows_hbm, rows))
        )
    ]
    for copy in copies:
        copy.start()
    copies[0].wait()
    copies[1].wait()
    route(ids_ref, owners_ref, pair_ref, rank_ref, label_ref, table_ref, slot_ref, pad, pairs, clusters)
    copies[2].wait()
    pack(slot_ref, label_ref, rows, blocks, numbers, capacity)


def first_blocks(ids, owners, rows, numbers, pairs, capacity):
    clusters = owners.shape[1]
    padded = -(-clusters // LANES) * LANES
    height = rows.shape[1] // LANES * capacity + EXTRA
    return pl.pallas_call(
        functools.partial(
            first_kernel, numbers=numbers, pairs=pairs, capacity=capacity, clusters=clusters
        ),
        in_specs=[HBM] * 3,
        out_specs=[VMEM] * (len(numbers) + 6),
        out_shape=[pltpu.VMEM((height, LANES), BF16)] * len(numbers)
        + [
            pltpu.VMEM(ids.shape, jnp.int32),
            pltpu.VMEM(ids.shape, jnp.int32),
            pltpu.VMEM(ids.shape, F32),
            pltpu.VMEM((8, padded), jnp.int32),
            pltpu.VMEM((pairs * ids.shape[0], LANES), F32),
            pltpu.VMEM(rows.shape, BF16),
        ],
        scratch_shapes=[
            pltpu.VMEM(ids.shape, jnp.int32),
            pltpu.VMEM(owners.shape, jnp.int32),
            pltpu.VMEM((8, padded), jnp.int32),
            pltpu.SemaphoreType.DMA((3,)),
        ],
        name="first",
        compiler_params=PARAMS,
    )(far(ids), far(owners), far(rows))


def later_kernel(slot_ref, label_ref, rows_ref, *blocks, numbers, capacity):
    pack(slot_ref, label_ref, rows_ref, blocks, numbers, capacity)


def later_blocks(slot, label, rows, numbers, capacity):
    height = rows.shape[1] // LANES * capacity + EXTRA
    return pl.pallas_call(
        functools.partial(later_kernel, numbers=numbers, capacity=capacity),
        in_specs=[VMEM] * 3,
        out_specs=[VMEM] * len(numbers),
        out_shape=[pltpu.VMEM((height, LANES), BF16)] * len(numbers),
        name="later",
        compiler_params=PARAMS,
    )(near(slot), near(label), near(rows))


def stage_kernel(*refs, old, new, capacity, width, last):
    slabs = width // LANES
    group = LANES // capacity
    total = old + new
    refs = list(refs)
    blocks = [refs.pop(0) for _ in range(2 * total)]
    best_in = refs.pop(0) if old else None
    out_ref, keys, marks = refs
    for b, block in enumerate(blocks):
        at = b * capacity
        for k in range(slabs):
            keys[at : at + capacity, k * LANES : (k + 1) * LANES] = block[
                k * capacity : (k + 1) * capacity, :
            ]
        marks[0:1, at : at + capacity] = block[
            slabs * capacity : slabs * capacity + EXTRA, 0:capacity
        ].astype(F32)[0:1, :]
    tiles, old_tiles = total // group, old // group
    best = [best_in[:, t * LANES : (t + 1) * LANES] for t in range(old_tiles)]
    best += [jnp.full((8, LANES), -1.0, F32)] * (tiles - old_tiles)

    def span(first, stop):
        return slice(first * LANES, stop * LANES)

    def visit(key_first, key_stop, first, stop):
        for left in range(key_first, key_stop, 2):
            right = min(left + 2, key_stop)
            gram = lax.dot_general(
                keys[span(left, right), :],
                keys[span(first, stop), :],
                (((1,), (1,)), ((), ())),
                preferred_element_type=F32,
            )
            for key in range(left, right):
                column = jnp.broadcast_to(marks[0:1, span(key, key + 1)], (LANES, LANES)).T
                for t in range(first, stop):
                    same = column == marks[0:1, span(t, t + 1)]
                    if t == key:
                        same = same & (iota((LANES, LANES), 0) != iota((LANES, LANES), 1))
                    piece = gram[span(key - left, key - left + 1), span(t - first, t - first + 1)]
                    piece = jnp.where(same, piece, -1.0)
                    top = jnp.max(piece.reshape(LANES // 8, 8, LANES), axis=0)
                    best[t] = jnp.maximum(best[t], top)

    visit(0, 2 * tiles, old_tiles, tiles)
    if old:
        visit(old_tiles, tiles, 0, old_tiles)
        visit(tiles + old_tiles, 2 * tiles, 0, old_tiles)
    if last is None:
        for t in range(tiles):
            out_ref[:, span(t, t + 1)] = best[t]
        return
    numbers, per_pair = last
    pairs = len(numbers)
    owner = lax.axis_index("owner")
    chip, core = owner // 2, owner % 2
    rows = [jnp.max(b, axis=0, keepdims=True) for b in best]
    row = jnp.concatenate(rows, axis=0)
    mark = jnp.concatenate([marks[0:1, span(t, t + 1)] for t in range(tiles)], axis=0)
    sums, counts = [], []
    for k in range(per_pair):
        mine = mark == k
        sums.append(jnp.sum(jnp.where(mine, row, 0.0), axis=0, keepdims=True))
        counts.append(jnp.sum(mine.astype(F32), axis=0, keepdims=True))
    stats = jnp.sum(jnp.concatenate(sums + counts, axis=0), axis=1, keepdims=True)
    stats = jnp.concatenate(
        [
            jnp.broadcast_to(stats, (2 * per_pair, LANES)),
            jnp.zeros((LANES - 2 * per_pair, LANES), F32),
        ],
        axis=0,
    ).T[0:1, :]
    for d in range(2 * pairs):
        out_ref[d, 1:2, :] = stats
    for t in range(tiles):
        marks[1:2, span(t, t + 1)] = rows[t]
    for b, m in enumerate(numbers):
        out_ref[2 * (chip ^ m) + core, 0:1, 0:capacity] = marks[
            1:2, b * capacity : (b + 1) * capacity
        ]


def stage(own, other, old, best, width, capacity, last):
    total = len(own)
    if last is None:
        out = pltpu.VMEM((8, total * capacity), F32)
    else:
        out = jax.ShapeDtypeStruct((2 * total, 8, LANES), F32)
    args = [near(b) for b in own] + [near(b) for b in other]
    if old:
        args.append(near(best))
    return pl.pallas_call(
        functools.partial(
            stage_kernel, old=old, new=total - old, capacity=capacity, width=width, last=last
        ),
        in_specs=[VMEM] * len(args),
        out_specs=VMEM,
        out_shape=out,
        scratch_shapes=[
            pltpu.VMEM((2 * total * capacity, width), BF16),
            pltpu.VMEM((8, 2 * total * capacity), F32),
        ],
        name="stage",
        compiler_params=PARAMS,
    )(*args)


def finish_kernel(back_ref, pair_ref, rank_ref, table_ref, maxima_ref, mean_ref, *, pairs, per_pair):
    core = lax.axis_index("owner") % 2
    pair, rank = pair_ref[...], rank_ref[...]
    maxima = jnp.zeros(pair.shape, F32)
    padded = table_ref.shape[1]
    pair_row, local_row = table_ref[0:1, :], table_ref[1:2, :]
    total = jnp.zeros((1, padded), F32)
    number = jnp.zeros((1, padded), F32)
    for p in range(pairs):
        got = lane_take(back_ref[2 * p + core, 0:1, :], rank)
        maxima = jnp.where(pair == p, got, maxima)
        stats = back_ref[2 * p, 1:2, :] + back_ref[2 * p + 1, 1:2, :]
        mine = pair_row == p
        index = jnp.where(mine, local_row, 0)
        parts = [index[:, f : f + LANES] for f in range(0, padded, LANES)]
        sums = jnp.concatenate([lane_take(stats, i) for i in parts], axis=1)
        counts = jnp.concatenate([lane_take(stats, i + per_pair) for i in parts], axis=1)
        total = jnp.where(mine, sums, total)
        number = jnp.where(mine, counts, number)
    maxima_ref[...] = maxima
    mean = total / jnp.maximum(number, 1.0)
    mean_ref[...] = mean[:, : mean_ref.shape[1]]


def finish(back, pair, rank, table, clusters, pairs, per_pair):
    return pl.pallas_call(
        functools.partial(finish_kernel, pairs=pairs, per_pair=per_pair),
        in_specs=[VMEM] * 4,
        out_specs=[VMEM] * 2,
        out_shape=[
            jax.ShapeDtypeStruct(pair.shape, F32),
            jax.ShapeDtypeStruct((1, clusters), F32),
        ],
        name="finish",
        compiler_params=PARAMS,
    )(back, near(pair), near(rank), near(table))


def plan(pairs):
    quarter = pairs // 4
    parts = [list(range(hi * quarter, (hi + 1) * quarter)) for hi in range(4)]
    sent = parts[3] + parts[2] + parts[1] + parts[0]
    stages = [parts[3] + parts[0][:1], parts[1] + parts[0][1:], parts[2]]
    return sent, quarter, stages


def body(embeddings, cluster_ids, owner_map):
    owners = lax.axis_size("owner")
    items, width = embeddings.shape
    clusters = owner_map.shape[0]
    pairs = owners // 2
    capacity = items // pairs
    per_pair = clusters // pairs
    ids = cluster_ids.reshape(items // LANES, LANES)
    sent, head, stages = plan(pairs)
    *blocks, pair, rank, label, table, slot, rows = first_blocks(
        ids, owner_map.reshape(1, clusters), embeddings, sent[:head], pairs, capacity
    )
    blocks += later_blocks(slot, label, rows, sent[head:], capacity)
    blocks = dict(zip(sent, blocks))
    swap = [(d, d ^ 1) for d in range(owners)]
    own = {}
    for m in sent:
        own[m] = blocks[m]
        if m:
            own[m] = lax.ppermute(own[m], "owner", [(d, d ^ (2 * m)) for d in range(owners)])
    other = {}
    done, best = [], None
    for index, new in enumerate(stages):
        for m in new:
            other[m] = lax.ppermute(own[m], "owner", swap)
        numbers = done + new
        last = (tuple(numbers), per_pair) if index == len(stages) - 1 else None
        best = stage(
            [own[m] for m in numbers],
            [other[m] for m in numbers],
            len(done),
            best,
            width,
            capacity,
            last,
        )
        done = numbers
    back = lax.all_to_all(best, "owner", split_axis=0, concat_axis=0, tiled=True)
    maxima, mean = finish(back, pair, rank, table, clusters, pairs, per_pair)
    return maxima.reshape(items), mean.reshape(clusters)


def solution(mesh):
    placed = (P(("parts", "owner"), None), P(("parts", "owner")), P("parts"))
    return jax.shard_map(
        body,
        mesh=mesh,
        in_specs=placed,
        out_specs=(P(("parts", "owner")), P("parts")),
        check_vma=False,
    )
```

```python
import functools

import jax
import jax.numpy as jnp
from jax import lax
from jax.experimental import pallas as pl
from jax.experimental.pallas import tpu as pltpu
from jax.sharding import PartitionSpec as P


LANES = 128
EXTRA = 8
F32 = jnp.float32
BF16 = jnp.bfloat16
VMEM = pl.BlockSpec(memory_space=pltpu.VMEM)
HBM = pl.BlockSpec(memory_space=pltpu.HBM)
PARAMS = pltpu.CompilerParams(vmem_limit_bytes=16 * 2**20)


def iota(shape, dim):
    return lax.broadcasted_iota(jnp.int32, shape, dim)


def near(value):
    return pltpu.with_memory_space_constraint(value, pltpu.VMEM)


def far(value):
    return pltpu.with_memory_space_constraint(value, pltpu.HBM)


def lane_take(row, index):
    if index.shape[0] == 1:
        return lane_take(row, jnp.broadcast_to(index, (8, LANES)))[0:1, :]
    out = None
    for first in range(0, row.shape[1], LANES):
        piece = jnp.broadcast_to(row[:, first : first + LANES], index.shape)
        local = index - first
        inside = (local >= 0) & (local < LANES)
        taken = jnp.take_along_axis(
            piece, jnp.where(inside, local, 0), axis=1, mode="promise_in_bounds"
        )
        out = taken if out is None else jnp.where(inside, taken, out)
    return out


def route(ids_ref, owners_ref, pair_ref, rank_ref, label_ref, table_ref, slot_ref, pad, pairs, clusters):
    chip = lax.axis_index("owner") // 2
    chunks = ids_ref.shape[0]
    padded = pad.shape[1]
    pad[...] = jnp.full(pad.shape, -2, jnp.int32)
    pad[0:1, 0:clusters] = owners_ref[...]
    pair_row = pad[0:1, :] >> 1
    across = jnp.broadcast_to(pair_row, (padded, padded))
    down = across.astype(F32).T.astype(jnp.int32)
    before = (across == down) & (iota(across.shape, 0) < iota(across.shape, 1))
    local_row = jnp.sum(before.astype(F32), axis=0, keepdims=True).astype(jnp.int32)
    table_ref[0:1, :] = pair_row
    table_ref[1:2, :] = local_row
    ids = ids_ref[...]
    pair = lane_take(pair_row, ids)
    label_ref[...] = lane_take(local_row, ids).astype(F32)
    hots = [pair == (chip ^ m) for m in range(pairs)]
    hot = jnp.concatenate([h.astype(F32) for h in hots], axis=0)
    upper = (iota((LANES, LANES), 0) <= iota((LANES, LANES), 1)).astype(BF16)
    within = jnp.dot(hot.astype(BF16), upper, preferred_element_type=F32)
    sums = jnp.dot(hot.astype(BF16), jnp.ones((LANES, LANES), BF16), preferred_element_type=F32)
    r, c = iota((pairs * chunks,) * 2, 0), iota((pairs * chunks,) * 2, 1)
    earlier = ((r // chunks == c // chunks) & (c < r)).astype(BF16)
    offset = jnp.dot(earlier, sums.astype(BF16), preferred_element_type=F32)
    slot = jnp.where(hot > 0.0, within + offset - 1.0, -1.0)
    item_rank = slot[0:chunks, :]
    for m in range(1, pairs):
        item_rank = jnp.maximum(item_rank, slot[m * chunks : (m + 1) * chunks, :])
    slot_ref[...] = slot
    pair_ref[...] = pair
    rank_ref[...] = item_rank.astype(jnp.int32)


def pack(slot_ref, label_ref, rows, blocks, numbers, capacity):
    chunks = label_ref.shape[0]
    width = rows.shape[1]
    slabs = width // LANES
    label = jnp.concatenate([label_ref[k : k + 1, :] for k in range(chunks)], axis=1)
    label = jnp.broadcast_to(label, (16, chunks * LANES)).astype(BF16)
    place = iota((capacity, LANES), 0).astype(F32)
    for block, m in zip(blocks, numbers):
        chosen = jnp.concatenate(
            [
                (place == slot_ref[m * chunks + k : m * chunks + k + 1, :]).astype(F32).astype(BF16)
                for k in range(chunks)
            ],
            axis=1,
        )
        values = jnp.dot(chosen, rows[...], preferred_element_type=F32)
        scale = lax.rsqrt(jnp.mean(values * values, axis=1, keepdims=True) + 1e-06)
        unit = (values * scale * (1.0 / jnp.sqrt(F32(width)))).astype(BF16)
        labels = lax.dot_general(
            label, chosen, (((1,), (1,)), ((), ())), preferred_element_type=F32
        )
        for k in range(slabs):
            block[k * capacity : (k + 1) * capacity, :] = unit[:, k * LANES : (k + 1) * LANES]
        block[slabs * capacity : slabs * capacity + EXTRA, 0:capacity] = labels.astype(BF16)[0:EXTRA, :]


def first_kernel(ids_hbm, owners_hbm, rows_hbm, *refs, numbers, pairs, capacity, clusters):
    n = len(numbers)
    blocks = refs[:n]
    pair_ref, rank_ref, label_ref, table_ref, slot_ref, rows, ids_ref, owners_ref, pad, sems = refs[n:]
    copies = [
        pltpu.make_async_copy(source, target, sems.at[k])
        for k, (source, target) in enumerate(
            ((ids_hbm, ids_ref), (owners_hbm, owners_ref), (rows_hbm, rows))
        )
    ]
    for copy in copies:
        copy.start()
    copies[0].wait()
    copies[1].wait()
    route(ids_ref, owners_ref, pair_ref, rank_ref, label_ref, table_ref, slot_ref, pad, pairs, clusters)
    copies[2].wait()
    pack(slot_ref, label_ref, rows, blocks, numbers, capacity)


def first_blocks(ids, owners, rows, numbers, pairs, capacity):
    clusters = owners.shape[1]
    padded = -(-clusters // LANES) * LANES
    height = rows.shape[1] // LANES * capacity + EXTRA
    return pl.pallas_call(
        functools.partial(
            first_kernel, numbers=numbers, pairs=pairs, capacity=capacity, clusters=clusters
        ),
        in_specs=[HBM] * 3,
        out_specs=[VMEM] * (len(numbers) + 6),
        out_shape=[pltpu.VMEM((height, LANES), BF16)] * len(numbers)
        + [
            pltpu.VMEM(ids.shape, jnp.int32),
            pltpu.VMEM(ids.shape, jnp.int32),
            pltpu.VMEM(ids.shape, F32),
            pltpu.VMEM((8, padded), jnp.int32),
            pltpu.VMEM((pairs * ids.shape[0], LANES), F32),
            pltpu.VMEM(rows.shape, BF16),
        ],
        scratch_shapes=[
            pltpu.VMEM(ids.shape, jnp.int32),
            pltpu.VMEM(owners.shape, jnp.int32),
            pltpu.VMEM((8, padded), jnp.int32),
            pltpu.SemaphoreType.DMA((3,)),
        ],
        name="first",
        compiler_params=PARAMS,
    )(far(ids), far(owners), far(rows))


def later_kernel(slot_ref, label_ref, rows_ref, *blocks, numbers, capacity):
    pack(slot_ref, label_ref, rows_ref, blocks, numbers, capacity)


def later_blocks(slot, label, rows, numbers, capacity):
    height = rows.shape[1] // LANES * capacity + EXTRA
    return pl.pallas_call(
        functools.partial(later_kernel, numbers=numbers, capacity=capacity),
        in_specs=[VMEM] * 3,
        out_specs=[VMEM] * len(numbers),
        out_shape=[pltpu.VMEM((height, LANES), BF16)] * len(numbers),
        name="later",
        compiler_params=PARAMS,
    )(near(slot), near(label), near(rows))


def span(first, stop):
    return slice(first * LANES, stop * LANES)


def place(block, keys, marks, at, capacity):
    slabs = keys.shape[1] // LANES
    for k in range(slabs):
        keys[at : at + capacity, k * LANES : (k + 1) * LANES] = block[
            k * capacity : (k + 1) * capacity, :
        ]
    marks[0:1, at : at + capacity] = block[
        slabs * capacity : slabs * capacity + EXTRA, 0:capacity
    ].astype(F32)[0:1, :]


def stage_kernel(*refs, own, other, fresh, items, capacity, last):
    refs = list(refs)
    blocks = [refs.pop(0) for _ in range(own[1] - own[0] + other[1] - other[0])]
    if not fresh:
        refs = refs[3:]
    keys, marks, state = refs[:3]
    starts = [b * capacity for b in range(*own)] + [items + b * capacity for b in range(*other)]
    for block, at in zip(blocks, starts):
        place(block, keys, marks, at, capacity)
    group, tiles = LANES // capacity, items // LANES
    old, total = (n // group for n in own)
    old_other, total_other = (tiles + n // group for n in other)
    best = {t: state[:, span(t, t + 1)] for t in range(old)}
    best |= {t: jnp.full((8, LANES), -1.0, F32) for t in range(old, total)}

    def meet(left, right, first, stop):
        if first == stop:
            return
        for low in range(left, right, 2):
            high = min(low + 2, right)
            gram = lax.dot_general(
                keys[span(low, high), :],
                keys[span(first, stop), :],
                (((1,), (1,)), ((), ())),
                preferred_element_type=F32,
            )
            for key in range(low, high):
                column = jnp.broadcast_to(marks[0:1, span(key, key + 1)], (LANES, LANES)).T
                for t in range(first, stop):
                    same = column == marks[0:1, span(t, t + 1)]
                    if t == key:
                        same = same & (iota((LANES, LANES), 0) != iota((LANES, LANES), 1))
                    piece = gram[span(key - low, key - low + 1), span(t - first, t - first + 1)]
                    piece = jnp.where(same, piece, -1.0)
                    top = jnp.max(piece.reshape(LANES // 8, 8, LANES), axis=0)
                    best[t] = jnp.maximum(best[t], top)

    meet(0, total, old, total)
    meet(tiles, total_other, old, total)
    meet(old, total, 0, old)
    meet(old_other, total_other, 0, old)
    if last is None:
        for t in range(total):
            state[:, span(t, t + 1)] = best[t]
    else:
        settle(best, marks, refs[3], capacity, **last)


def settle(best, marks, out_ref, capacity, numbers, per_pair):
    pairs, tiles = len(numbers), len(best)
    owner = lax.axis_index("owner")
    chip, core = owner // 2, owner % 2
    rows = [jnp.max(best[t], axis=0, keepdims=True) for t in range(tiles)]
    row = jnp.concatenate(rows, axis=0)
    mark = jnp.concatenate([marks[0:1, span(t, t + 1)] for t in range(tiles)], axis=0)
    sums, counts = [], []
    for k in range(per_pair):
        mine = mark == k
        sums.append(jnp.sum(jnp.where(mine, row, 0.0), axis=0, keepdims=True))
        counts.append(jnp.sum(mine.astype(F32), axis=0, keepdims=True))
    stats = jnp.sum(jnp.concatenate(sums + counts, axis=0), axis=1, keepdims=True)
    stats = jnp.where(iota((2 * per_pair, LANES), 0) == iota((2 * per_pair, LANES), 1), stats, 0.0)
    stats = jnp.sum(stats, axis=0, keepdims=True)
    out_ref[:, span(1, 2)] = jnp.broadcast_to(stats, (2 * pairs, LANES))
    target = iota((2 * pairs, LANES), 0)
    back = jnp.zeros((2 * pairs, LANES), F32)
    for b, m in enumerate(numbers):
        line, shift = rows[b * capacity // LANES], b * capacity % LANES
        if shift:
            line = pltpu.roll(jnp.broadcast_to(line, (8, LANES)), LANES - shift, 1)[0:1, :]
        back = jnp.where(target == 2 * (chip ^ m) + core, line, back)
    out_ref[:, span(0, 1)] = back


def stage(new_own, new_other, own, other, state, items, width, capacity, last):
    args = [near(b) for b in new_own + new_other]
    fresh = state is None
    out = [
        pltpu.VMEM((2 * items, width), BF16),
        pltpu.VMEM((8, 2 * items), F32),
        pltpu.VMEM((8, items), F32),
    ]
    aliases = {} if fresh else {len(args) + k: k for k in range(3)}
    args += [] if fresh else [near(a) for a in state]
    if last is not None:
        out.append(pltpu.VMEM((2 * len(last["numbers"]), 2 * LANES), F32))
    return pl.pallas_call(
        functools.partial(
            stage_kernel,
            own=own,
            other=other,
            fresh=fresh,
            items=items,
            capacity=capacity,
            last=last,
        ),
        in_specs=[VMEM] * len(args),
        out_specs=[VMEM] * len(out),
        out_shape=out,
        input_output_aliases=aliases,
        name="stage",
        compiler_params=PARAMS,
    )(*args)


def finish_kernel(back_ref, pair_ref, rank_ref, table_ref, maxima_ref, mean_ref, *, pairs, per_pair):
    core = lax.axis_index("owner") % 2
    pair, rank = pair_ref[...], rank_ref[...]
    maxima = jnp.zeros(pair.shape, F32)
    padded = table_ref.shape[1]
    pair_row, local_row = table_ref[0:1, :], table_ref[1:2, :]
    total = jnp.zeros((1, padded), F32)
    number = jnp.zeros((1, padded), F32)
    for p in range(pairs):
        got = jnp.where(core == 0, back_ref[2 * p : 2 * p + 1, span(0, 1)], back_ref[2 * p + 1 : 2 * p + 2, span(0, 1)])
        got = lane_take(got, rank)
        maxima = jnp.where(pair == p, got, maxima)
        stats = back_ref[2 * p : 2 * p + 1, span(1, 2)] + back_ref[2 * p + 1 : 2 * p + 2, span(1, 2)]
        mine = pair_row == p
        index = jnp.where(mine, local_row, 0)
        parts = [index[:, f : f + LANES] for f in range(0, padded, LANES)]
        sums = jnp.concatenate([lane_take(stats, i) for i in parts], axis=1)
        counts = jnp.concatenate([lane_take(stats, i + per_pair) for i in parts], axis=1)
        total = jnp.where(mine, sums, total)
        number = jnp.where(mine, counts, number)
    maxima_ref[...] = maxima
    mean = total / jnp.maximum(number, 1.0)
    mean_ref[...] = mean[:, : mean_ref.shape[1]]


def finish(back, pair, rank, table, clusters, pairs, per_pair):
    return pl.pallas_call(
        functools.partial(finish_kernel, pairs=pairs, per_pair=per_pair),
        in_specs=[VMEM] * 4,
        out_specs=[VMEM] * 2,
        out_shape=[
            jax.ShapeDtypeStruct(pair.shape, F32),
            jax.ShapeDtypeStruct((1, clusters), F32),
        ],
        name="finish",
        compiler_params=PARAMS,
    )(near(back), near(pair), near(rank), near(table))


def plan(pairs):
    size = pairs // 8
    part = [list(range(k * size, (k + 1) * size)) for k in range(8)]
    sent = part[6] + part[7] + part[4] + part[5] + part[2] + part[3] + part[1] + part[0]
    stages = [part[0] + part[6] + part[2], part[3] + part[1], part[7], part[4], part[5]]
    return sent, 2 * size, stages, part[0]


def body(embeddings, cluster_ids, owner_map):
    owners = lax.axis_size("owner")
    items, width = embeddings.shape
    clusters = owner_map.shape[0]
    pairs = owners // 2
    capacity = items // pairs
    per_pair = clusters // pairs
    ids = cluster_ids.reshape(items // LANES, LANES)
    sent, head, stages, local = plan(pairs)
    *blocks, pair, rank, label, table, slot, rows = first_blocks(
        ids, owner_map.reshape(1, clusters), embeddings, sent[:head], pairs, capacity
    )
    blocks += later_blocks(slot, label, rows, sent[head:], capacity)
    blocks = dict(zip(sent, blocks))
    swap = [(d, d ^ 1) for d in range(owners)]
    own, other = {}, {}
    for m in sent:
        own[m] = blocks[m]
        if m:
            own[m] = lax.ppermute(own[m], "owner", [(d, d ^ (2 * m)) for d in range(owners)])
    order = tuple(m for new in stages for m in new)
    for m in order:
        other[m] = lax.ppermute(own[m], "owner", swap)
    state, mine, theirs = None, 0, 0
    waiting = local
    for new in stages + [[]]:
        last = None if new else dict(numbers=order, per_pair=per_pair)
        own_range, other_range = (mine, mine + len(new)), (theirs, theirs + len(waiting))
        result = stage(
            [own[m] for m in new],
            [other[m] for m in waiting],
            own_range,
            other_range,
            state,
            items,
            width,
            capacity,
            last,
        )
        state = result[:3]
        mine, theirs = own_range[1], other_range[1]
        waiting = list(order[theirs:mine])
    back = lax.all_to_all(result[3], "owner", split_axis=0, concat_axis=0, tiled=True)
    maxima, mean = finish(back, pair, rank, table, clusters, pairs, per_pair)
    return maxima.reshape(items), mean.reshape(clusters)


def solution(mesh):
    placed = (P(("parts", "owner"), None), P(("parts", "owner")), P("parts"))
    return jax.shard_map(
        body,
        mesh=mesh,
        in_specs=placed,
        out_specs=(P(("parts", "owner")), P("parts")),
        check_vma=False,
    )
```

```python
import functools

import jax
import jax.numpy as jnp
from jax import lax
from jax.experimental import pallas as pl
from jax.experimental.pallas import tpu as pltpu
from jax.sharding import PartitionSpec as P


LANES = 128
EXTRA = 8
CHUNKS = 4
F32 = jnp.float32
BF16 = jnp.bfloat16
VMEM = pl.BlockSpec(memory_space=pltpu.VMEM)
HBM = pl.BlockSpec(memory_space=pltpu.HBM)
PARAMS = pltpu.CompilerParams(vmem_limit_bytes=16 * 2**20)


def iota(shape, dim):
    return lax.broadcasted_iota(jnp.int32, shape, dim)


def near(value):
    return pltpu.with_memory_space_constraint(value, pltpu.VMEM)


def far(value):
    return pltpu.with_memory_space_constraint(value, pltpu.HBM)


def lane_take(row, index):
    if index.shape[0] == 1:
        return lane_take(row, jnp.broadcast_to(index, (8, LANES)))[0:1, :]
    out = None
    for first in range(0, row.shape[1], LANES):
        piece = jnp.broadcast_to(row[:, first : first + LANES], index.shape)
        local = index - first
        inside = (local >= 0) & (local < LANES)
        taken = jnp.take_along_axis(
            piece, jnp.where(inside, local, 0), axis=1, mode="promise_in_bounds"
        )
        out = taken if out is None else jnp.where(inside, taken, out)
    return out


def route(ids_ref, owners_ref, pair_ref, rank_ref, label_ref, table_ref, slot_ref, pad, pairs, clusters):
    chip = lax.axis_index("owner") // 2
    chunks = ids_ref.shape[0]
    padded = pad.shape[1]
    pad[...] = jnp.full(pad.shape, -2, jnp.int32)
    pad[0:1, 0:clusters] = owners_ref[...]
    pair_row = pad[0:1, :] >> 1
    across = jnp.broadcast_to(pair_row, (padded, padded))
    down = across.astype(F32).T.astype(jnp.int32)
    before = (across == down) & (iota(across.shape, 0) < iota(across.shape, 1))
    local_row = jnp.sum(before.astype(F32), axis=0, keepdims=True).astype(jnp.int32)
    table_ref[0:1, :] = pair_row
    table_ref[1:2, :] = local_row
    ids = ids_ref[...]
    pair = lane_take(pair_row, ids)
    label_ref[...] = lane_take(local_row, ids).astype(F32)
    hots = [pair == (chip ^ m) for m in range(pairs)]
    hot = jnp.concatenate([h.astype(F32) for h in hots], axis=0)
    upper = (iota((LANES, LANES), 0) <= iota((LANES, LANES), 1)).astype(BF16)
    within = jnp.dot(hot.astype(BF16), upper, preferred_element_type=F32)
    sums = jnp.dot(hot.astype(BF16), jnp.ones((LANES, LANES), BF16), preferred_element_type=F32)
    r, c = iota((pairs * chunks,) * 2, 0), iota((pairs * chunks,) * 2, 1)
    earlier = ((r // chunks == c // chunks) & (c < r)).astype(BF16)
    offset = jnp.dot(earlier, sums.astype(BF16), preferred_element_type=F32)
    slot = jnp.where(hot > 0.0, within + offset - 1.0, -1.0)
    item_rank = slot[0:chunks, :]
    for m in range(1, pairs):
        item_rank = jnp.maximum(item_rank, slot[m * chunks : (m + 1) * chunks, :])
    slot_ref[...] = slot
    pair_ref[...] = pair
    rank_ref[...] = item_rank.astype(jnp.int32)


def pack(slot_ref, label_ref, rows, blocks, numbers, capacity, arrived=None):
    chunks = label_ref.shape[0]
    width = rows.shape[1]
    slabs = width // LANES
    label = jnp.concatenate([label_ref[k : k + 1, :] for k in range(chunks)], axis=1)
    label = jnp.broadcast_to(label, (16, chunks * LANES)).astype(BF16)
    place = iota((capacity, LANES), 0).astype(F32)
    for block, m in zip(blocks, numbers):
        chosen = jnp.concatenate(
            [
                (place == slot_ref[m * chunks + k : m * chunks + k + 1, :]).astype(F32).astype(BF16)
                for k in range(chunks)
            ],
            axis=1,
        )
        if arrived is None:
            values = jnp.dot(chosen, rows[...], preferred_element_type=F32)
        else:
            values = jnp.zeros((capacity, width), F32)
            step = rows.shape[0] // len(arrived)
            for k, copy in enumerate(arrived):
                if block is blocks[0]:
                    copy.wait()
                piece = slice(k * step, (k + 1) * step)
                values += jnp.dot(chosen[:, piece], rows[piece, :], preferred_element_type=F32)
        scale = lax.rsqrt(jnp.mean(values * values, axis=1, keepdims=True) + 1e-06)
        unit = (values * scale * (1.0 / jnp.sqrt(F32(width)))).astype(BF16)
        labels = lax.dot_general(
            label, chosen, (((1,), (1,)), ((), ())), preferred_element_type=F32
        )
        for k in range(slabs):
            block[k * capacity : (k + 1) * capacity, :] = unit[:, k * LANES : (k + 1) * LANES]
        block[slabs * capacity : slabs * capacity + EXTRA, 0:capacity] = labels.astype(BF16)[0:EXTRA, :]


def first_kernel(ids_hbm, owners_hbm, rows_hbm, *refs, numbers, pairs, capacity, clusters):
    n = len(numbers)
    blocks = refs[:n]
    pair_ref, rank_ref, label_ref, table_ref, slot_ref, rows, ids_ref, owners_ref, pad, sems = refs[n:]
    step = rows.shape[0] // CHUNKS
    copies = [(ids_hbm, ids_ref), (owners_hbm, owners_ref)]
    for k in range(CHUNKS):
        piece = pl.ds(k * step, step)
        copies.append((rows_hbm.at[piece, :], rows.at[piece, :]))
    copies = [
        pltpu.make_async_copy(source, target, sems.at[k])
        for k, (source, target) in enumerate(copies)
    ]
    for copy in copies:
        copy.start()
    copies[0].wait()
    copies[1].wait()
    route(ids_ref, owners_ref, pair_ref, rank_ref, label_ref, table_ref, slot_ref, pad, pairs, clusters)
    pack(slot_ref, label_ref, rows, blocks, numbers, capacity, copies[2:])


def first_blocks(ids, owners, rows, numbers, pairs, capacity):
    clusters = owners.shape[1]
    padded = -(-clusters // LANES) * LANES
    height = rows.shape[1] // LANES * capacity + EXTRA
    return pl.pallas_call(
        functools.partial(
            first_kernel, numbers=numbers, pairs=pairs, capacity=capacity, clusters=clusters
        ),
        in_specs=[HBM] * 3,
        out_specs=[VMEM] * (len(numbers) + 6),
        out_shape=[pltpu.VMEM((height, LANES), BF16)] * len(numbers)
        + [
            pltpu.VMEM(ids.shape, jnp.int32),
            pltpu.VMEM(ids.shape, jnp.int32),
            pltpu.VMEM(ids.shape, F32),
            pltpu.VMEM((8, padded), jnp.int32),
            pltpu.VMEM((pairs * ids.shape[0], LANES), F32),
            pltpu.VMEM(rows.shape, BF16),
        ],
        scratch_shapes=[
            pltpu.VMEM(ids.shape, jnp.int32),
            pltpu.VMEM(owners.shape, jnp.int32),
            pltpu.VMEM((8, padded), jnp.int32),
            pltpu.SemaphoreType.DMA((2 + CHUNKS,)),
        ],
        name="first",
        compiler_params=PARAMS,
    )(far(ids), far(owners), far(rows))


def later_kernel(slot_ref, label_ref, rows_ref, *blocks, numbers, capacity):
    pack(slot_ref, label_ref, rows_ref, blocks, numbers, capacity)


def later_blocks(slot, label, rows, numbers, capacity):
    height = rows.shape[1] // LANES * capacity + EXTRA
    return pl.pallas_call(
        functools.partial(later_kernel, numbers=numbers, capacity=capacity),
        in_specs=[VMEM] * 3,
        out_specs=[VMEM] * len(numbers),
        out_shape=[pltpu.VMEM((height, LANES), BF16)] * len(numbers),
        name="later",
        compiler_params=PARAMS,
    )(near(slot), near(label), near(rows))


def span(first, stop):
    return slice(first * LANES, stop * LANES)


def place(block, keys, marks, at, capacity):
    slabs = keys.shape[1] // LANES
    for k in range(slabs):
        keys[at : at + capacity, k * LANES : (k + 1) * LANES] = block[
            k * capacity : (k + 1) * capacity, :
        ]
    marks[0:1, at : at + capacity] = block[
        slabs * capacity : slabs * capacity + EXTRA, 0:capacity
    ].astype(F32)[0:1, :]


def stage_kernel(*refs, own, other, fresh, items, capacity, last):
    refs = list(refs)
    blocks = [refs.pop(0) for _ in range(own[1] - own[0] + other[1] - other[0])]
    if not fresh:
        refs = refs[4:]
    keys, marks, columns, state = refs[:4]
    starts = [b * capacity for b in range(*own)] + [items + b * capacity for b in range(*other)]
    for block, at in zip(blocks, starts):
        place(block, keys, marks, at, capacity)
    group, tiles = LANES // capacity, items // LANES
    old, total = (n // group for n in own)
    old_other, total_other = (tiles + n // group for n in other)
    for t in [*range(old, total), *range(old_other, total_other)]:
        columns[span(t, t + 1), :] = jnp.broadcast_to(marks[0:1, span(t, t + 1)], (LANES, LANES)).T
    best = {t: state[:, span(t, t + 1)] for t in range(old)}
    best |= {t: jnp.full((8, LANES), -1.0, F32) for t in range(old, total)}

    def meet(left, right, first, stop):
        if first == stop:
            return
        step = max(2, 8 // (stop - first))
        for low in range(left, right, step):
            high = min(low + step, right)
            gram = lax.dot_general(
                keys[span(low, high), :],
                keys[span(first, stop), :],
                (((1,), (1,)), ((), ())),
                preferred_element_type=F32,
            )
            for key in range(low, high):
                column = columns[span(key, key + 1), :]
                for t in range(first, stop):
                    same = column == marks[0:1, span(t, t + 1)]
                    if t == key:
                        same = same & (iota((LANES, LANES), 0) != iota((LANES, LANES), 1))
                    piece = gram[span(key - low, key - low + 1), span(t - first, t - first + 1)]
                    piece = jnp.where(same, piece, -1.0)
                    top = jnp.max(piece.reshape(LANES // 8, 8, LANES), axis=0)
                    best[t] = jnp.maximum(best[t], top)

    meet(0, total, old, total)
    meet(tiles, total_other, old, total)
    meet(old, total, 0, old)
    meet(old_other, total_other, 0, old)
    if last is None:
        for t in range(total):
            state[:, span(t, t + 1)] = best[t]
    else:
        settle(best, marks, refs[4], capacity, **last)


def settle(best, marks, out_ref, capacity, numbers, per_pair):
    pairs, tiles = len(numbers), len(best)
    owner = lax.axis_index("owner")
    chip, core = owner // 2, owner % 2
    rows = [jnp.max(best[t], axis=0, keepdims=True) for t in range(tiles)]
    row = jnp.concatenate(rows, axis=0)
    mark = jnp.concatenate([marks[0:1, span(t, t + 1)] for t in range(tiles)], axis=0)
    sums, counts = [], []
    for k in range(per_pair):
        mine = mark == k
        sums.append(jnp.sum(jnp.where(mine, row, 0.0), axis=0, keepdims=True))
        counts.append(jnp.sum(mine.astype(F32), axis=0, keepdims=True))
    stats = jnp.sum(jnp.concatenate(sums + counts, axis=0), axis=1, keepdims=True)
    stats = jnp.where(iota((2 * per_pair, LANES), 0) == iota((2 * per_pair, LANES), 1), stats, 0.0)
    stats = jnp.sum(stats, axis=0, keepdims=True)
    out_ref[:, span(1, 2)] = jnp.broadcast_to(stats, (2 * pairs, LANES))
    target = iota((2 * pairs, LANES), 0)
    back = jnp.zeros((2 * pairs, LANES), F32)
    for b, m in enumerate(numbers):
        line, shift = rows[b * capacity // LANES], b * capacity % LANES
        if shift:
            line = pltpu.roll(jnp.broadcast_to(line, (8, LANES)), LANES - shift, 1)[0:1, :]
        back = jnp.where(target == 2 * (chip ^ m) + core, line, back)
    out_ref[:, span(0, 1)] = back


def stage(new_own, new_other, own, other, state, items, width, capacity, last):
    args = [near(b) for b in new_own + new_other]
    fresh = state is None
    out = [
        pltpu.VMEM((2 * items, width), BF16),
        pltpu.VMEM((8, 2 * items), F32),
        pltpu.VMEM((2 * items, LANES), F32),
        pltpu.VMEM((8, items), F32),
    ]
    aliases = {} if fresh else {len(args) + k: k for k in range(len(out))}
    args += [] if fresh else [near(a) for a in state]
    if last is not None:
        out.append(pltpu.VMEM((2 * len(last["numbers"]), 2 * LANES), F32))
    return pl.pallas_call(
        functools.partial(
            stage_kernel,
            own=own,
            other=other,
            fresh=fresh,
            items=items,
            capacity=capacity,
            last=last,
        ),
        in_specs=[VMEM] * len(args),
        out_specs=[VMEM] * len(out),
        out_shape=out,
        input_output_aliases=aliases,
        name="stage",
        compiler_params=PARAMS,
    )(*args)


def finish_kernel(back_ref, pair_ref, rank_ref, table_ref, maxima_ref, mean_ref, *, pairs, per_pair):
    core = lax.axis_index("owner") % 2
    pair, rank = pair_ref[...], rank_ref[...]
    maxima = jnp.zeros(pair.shape, F32)
    padded = table_ref.shape[1]
    pair_row, local_row = table_ref[0:1, :], table_ref[1:2, :]
    total = jnp.zeros((1, padded), F32)
    number = jnp.zeros((1, padded), F32)
    for p in range(pairs):
        got = jnp.where(core == 0, back_ref[2 * p : 2 * p + 1, span(0, 1)], back_ref[2 * p + 1 : 2 * p + 2, span(0, 1)])
        got = lane_take(got, rank)
        maxima = jnp.where(pair == p, got, maxima)
        stats = back_ref[2 * p : 2 * p + 1, span(1, 2)] + back_ref[2 * p + 1 : 2 * p + 2, span(1, 2)]
        mine = pair_row == p
        index = jnp.where(mine, local_row, 0)
        parts = [index[:, f : f + LANES] for f in range(0, padded, LANES)]
        sums = jnp.concatenate([lane_take(stats, i) for i in parts], axis=1)
        counts = jnp.concatenate([lane_take(stats, i + per_pair) for i in parts], axis=1)
        total = jnp.where(mine, sums, total)
        number = jnp.where(mine, counts, number)
    maxima_ref[...] = maxima
    mean = total / jnp.maximum(number, 1.0)
    mean_ref[...] = mean[:, : mean_ref.shape[1]]


def finish(back, pair, rank, table, clusters, pairs, per_pair):
    return pl.pallas_call(
        functools.partial(finish_kernel, pairs=pairs, per_pair=per_pair),
        in_specs=[VMEM] * 4,
        out_specs=[VMEM] * 2,
        out_shape=[
            jax.ShapeDtypeStruct(pair.shape, F32),
            jax.ShapeDtypeStruct((1, clusters), F32),
        ],
        name="finish",
        compiler_params=PARAMS,
    )(near(back), near(pair), near(rank), near(table))


def plan(pairs):
    size = pairs // 8
    part = [list(range(k * size, (k + 1) * size)) for k in range(8)]
    sent = part[6] + part[7] + part[4] + part[5] + part[2] + part[3] + part[1] + part[0]
    stages = [
        (part[0] + part[6] + part[2], part[0]),
        (part[3] + part[1], part[6] + part[2]),
        (part[7], part[3] + part[1]),
        (part[4], part[7]),
        ([], part[4]),
        (part[5], []),
        ([], part[5]),
    ]
    return sent, size, stages


def body(embeddings, cluster_ids, owner_map):
    owners = lax.axis_size("owner")
    items, width = embeddings.shape
    clusters = owner_map.shape[0]
    pairs = owners // 2
    capacity = items // pairs
    per_pair = clusters // pairs
    ids = cluster_ids.reshape(items // LANES, LANES)
    sent, head, stages = plan(pairs)
    *blocks, pair, rank, label, table, slot, rows = first_blocks(
        ids, owner_map.reshape(1, clusters), embeddings, sent[:head], pairs, capacity
    )
    blocks += later_blocks(slot, label, rows, sent[head:], capacity)
    blocks = dict(zip(sent, blocks))
    swap = [(d, d ^ 1) for d in range(owners)]
    own, other = {}, {}
    for m in sent:
        own[m] = blocks[m]
        if m:
            own[m] = lax.ppermute(own[m], "owner", [(d, d ^ (2 * m)) for d in range(owners)])
    order = tuple(m for new, _ in stages for m in new)
    for m in order:
        other[m] = lax.ppermute(own[m], "owner", swap)
    state, mine, theirs = None, 0, 0
    for index, (new, swapped) in enumerate(stages):
        final = index == len(stages) - 1
        state = stage(
            [own[m] for m in new],
            [other[m] for m in swapped],
            (mine, mine + len(new)),
            (theirs, theirs + len(swapped)),
            state,
            items,
            width,
            capacity,
            dict(numbers=order, per_pair=per_pair) if final else None,
        )
        mine, theirs = mine + len(new), theirs + len(swapped)
    back = lax.all_to_all(state[-1], "owner", split_axis=0, concat_axis=0, tiled=True)
    maxima, mean = finish(back, pair, rank, table, clusters, pairs, per_pair)
    return maxima.reshape(items), mean.reshape(clusters)


def solution(mesh):
    placed = (P(("parts", "owner"), None), P(("parts", "owner")), P("parts"))
    return jax.shard_map(
        body,
        mesh=mesh,
        in_specs=placed,
        out_specs=(P(("parts", "owner")), P("parts")),
        check_vma=False,
    )
```

```python
import functools

import jax
import jax.numpy as jnp
from jax import lax
from jax.experimental import pallas as pl
from jax.experimental.pallas import tpu as pltpu
from jax.sharding import PartitionSpec as P


LANES = 128
EXTRA = 8
CHUNKS = 4
F32 = jnp.float32
BF16 = jnp.bfloat16
VMEM = pl.BlockSpec(memory_space=pltpu.VMEM)
HBM = pl.BlockSpec(memory_space=pltpu.HBM)
PARAMS = pltpu.CompilerParams(vmem_limit_bytes=16 * 2**20)


def iota(shape, dim):
    return lax.broadcasted_iota(jnp.int32, shape, dim)


def near(value):
    return pltpu.with_memory_space_constraint(value, pltpu.VMEM)


def far(value):
    return pltpu.with_memory_space_constraint(value, pltpu.HBM)


def lane_take(row, index):
    if index.shape[0] == 1:
        return lane_take(row, jnp.broadcast_to(index, (8, LANES)))[0:1, :]
    out = None
    for first in range(0, row.shape[1], LANES):
        piece = jnp.broadcast_to(row[:, first : first + LANES], index.shape)
        local = index - first
        inside = (local >= 0) & (local < LANES)
        taken = jnp.take_along_axis(
            piece, jnp.where(inside, local, 0), axis=1, mode="promise_in_bounds"
        )
        out = taken if out is None else jnp.where(inside, taken, out)
    return out


def route(ids_ref, owners_ref, pair_ref, rank_ref, label_ref, table_ref, slot_ref, pad, pairs, clusters):
    chip = lax.axis_index("owner") // 2
    chunks = ids_ref.shape[0]
    padded = pad.shape[1]
    pad[...] = jnp.full(pad.shape, -2, jnp.int32)
    pad[0:1, 0:clusters] = owners_ref[...]
    pair_row = pad[0:1, :] >> 1
    across = jnp.broadcast_to(pair_row, (padded, padded))
    down = across.astype(F32).T.astype(jnp.int32)
    before = (across == down) & (iota(across.shape, 0) < iota(across.shape, 1))
    local_row = jnp.sum(before.astype(F32), axis=0, keepdims=True).astype(jnp.int32)
    table_ref[0:1, :] = pair_row
    table_ref[1:2, :] = local_row
    ids = ids_ref[...]
    pair = lane_take(pair_row, ids)
    label_ref[...] = lane_take(local_row, ids).astype(F32)
    hots = [pair == (chip ^ m) for m in range(pairs)]
    hot = jnp.concatenate([h.astype(F32) for h in hots], axis=0)
    upper = (iota((LANES, LANES), 0) <= iota((LANES, LANES), 1)).astype(BF16)
    within = jnp.dot(hot.astype(BF16), upper, preferred_element_type=F32)
    sums = jnp.dot(hot.astype(BF16), jnp.ones((LANES, LANES), BF16), preferred_element_type=F32)
    r, c = iota((pairs * chunks,) * 2, 0), iota((pairs * chunks,) * 2, 1)
    earlier = ((r // chunks == c // chunks) & (c < r)).astype(BF16)
    offset = jnp.dot(earlier, sums.astype(BF16), preferred_element_type=F32)
    slot = jnp.where(hot > 0.0, within + offset - 1.0, -1.0)
    item_rank = slot[0:chunks, :]
    for m in range(1, pairs):
        item_rank = jnp.maximum(item_rank, slot[m * chunks : (m + 1) * chunks, :])
    slot_ref[...] = slot
    pair_ref[...] = pair
    rank_ref[...] = item_rank.astype(jnp.int32)


def pack(slot_ref, label_ref, rows, blocks, numbers, capacity, arrived=None):
    chunks = label_ref.shape[0]
    width = rows.shape[1]
    slabs = width // LANES
    label = jnp.concatenate([label_ref[k : k + 1, :] for k in range(chunks)], axis=1)
    label = jnp.broadcast_to(label, (16, chunks * LANES)).astype(BF16)
    place = iota((capacity, LANES), 0).astype(F32)
    for block, m in zip(blocks, numbers):
        chosen = jnp.concatenate(
            [
                (place == slot_ref[m * chunks + k : m * chunks + k + 1, :]).astype(F32).astype(BF16)
                for k in range(chunks)
            ],
            axis=1,
        )
        if arrived is None:
            values = jnp.dot(chosen, rows[...], preferred_element_type=F32)
        else:
            values = jnp.zeros((capacity, width), F32)
            step = rows.shape[0] // len(arrived)
            for k, copy in enumerate(arrived):
                if block is blocks[0]:
                    copy.wait()
                piece = slice(k * step, (k + 1) * step)
                values += jnp.dot(chosen[:, piece], rows[piece, :], preferred_element_type=F32)
        scale = lax.rsqrt(jnp.mean(values * values, axis=1, keepdims=True) + 1e-06)
        unit = (values * scale * (1.0 / jnp.sqrt(F32(width)))).astype(BF16)
        labels = lax.dot_general(
            label, chosen, (((1,), (1,)), ((), ())), preferred_element_type=F32
        )
        for k in range(slabs):
            block[k * capacity : (k + 1) * capacity, :] = unit[:, k * LANES : (k + 1) * LANES]
        block[slabs * capacity : slabs * capacity + EXTRA, 0:capacity] = labels.astype(BF16)[0:EXTRA, :]


def first_kernel(ids_hbm, owners_hbm, rows_hbm, *refs, numbers, pairs, capacity, clusters):
    n = len(numbers)
    blocks = refs[:n]
    pair_ref, rank_ref, label_ref, table_ref, slot_ref, rows, ids_ref, owners_ref, pad, sems = refs[n:]
    step = rows.shape[0] // CHUNKS
    copies = [(ids_hbm, ids_ref), (owners_hbm, owners_ref)]
    for k in range(CHUNKS):
        piece = pl.ds(k * step, step)
        copies.append((rows_hbm.at[piece, :], rows.at[piece, :]))
    copies = [
        pltpu.make_async_copy(source, target, sems.at[k])
        for k, (source, target) in enumerate(copies)
    ]
    for copy in copies:
        copy.start()
    copies[0].wait()
    copies[1].wait()
    route(ids_ref, owners_ref, pair_ref, rank_ref, label_ref, table_ref, slot_ref, pad, pairs, clusters)
    pack(slot_ref, label_ref, rows, blocks, numbers, capacity, copies[2:])


def first_blocks(ids, owners, rows, numbers, pairs, capacity):
    clusters = owners.shape[1]
    padded = -(-clusters // LANES) * LANES
    height = rows.shape[1] // LANES * capacity + EXTRA
    return pl.pallas_call(
        functools.partial(
            first_kernel, numbers=numbers, pairs=pairs, capacity=capacity, clusters=clusters
        ),
        in_specs=[HBM] * 3,
        out_specs=[VMEM] * (len(numbers) + 6),
        out_shape=[pltpu.VMEM((height, LANES), BF16)] * len(numbers)
        + [
            pltpu.VMEM(ids.shape, jnp.int32),
            pltpu.VMEM(ids.shape, jnp.int32),
            pltpu.VMEM(ids.shape, F32),
            pltpu.VMEM((8, padded), jnp.int32),
            pltpu.VMEM((pairs * ids.shape[0], LANES), F32),
            pltpu.VMEM(rows.shape, BF16),
        ],
        scratch_shapes=[
            pltpu.VMEM(ids.shape, jnp.int32),
            pltpu.VMEM(owners.shape, jnp.int32),
            pltpu.VMEM((8, padded), jnp.int32),
            pltpu.SemaphoreType.DMA((2 + CHUNKS,)),
        ],
        name="first",
        compiler_params=PARAMS,
    )(far(ids), far(owners), far(rows))


def later_kernel(slot_ref, label_ref, rows_ref, *blocks, numbers, capacity):
    pack(slot_ref, label_ref, rows_ref, blocks, numbers, capacity)


def later_blocks(slot, label, rows, numbers, capacity):
    height = rows.shape[1] // LANES * capacity + EXTRA
    return pl.pallas_call(
        functools.partial(later_kernel, numbers=numbers, capacity=capacity),
        in_specs=[VMEM] * 3,
        out_specs=[VMEM] * len(numbers),
        out_shape=[pltpu.VMEM((height, LANES), BF16)] * len(numbers),
        name="later",
        compiler_params=PARAMS,
    )(near(slot), near(label), near(rows))


def span(first, stop):
    return slice(first * LANES, stop * LANES)


def place(block, keys, marks, at, capacity):
    slabs = keys.shape[1] // LANES
    for k in range(slabs):
        keys[at : at + capacity, k * LANES : (k + 1) * LANES] = block[
            k * capacity : (k + 1) * capacity, :
        ]
    marks[0:1, at : at + capacity] = block[
        slabs * capacity : slabs * capacity + EXTRA, 0:capacity
    ].astype(F32)[0:1, :]


def stage_kernel(*refs, own, other, fresh, items, capacity, per_pair, last):
    refs = list(refs)
    blocks = [refs.pop(0) for _ in range(own[1] - own[0] + other[1] - other[0])]
    if not fresh:
        refs = refs[4:]
    keys, marks, columns, state = refs[:4]
    starts = [b * capacity for b in range(*own)] + [items + b * capacity for b in range(*other)]
    for block, at in zip(blocks, starts):
        place(block, keys, marks, at, capacity)
    group, tiles = LANES // capacity, items // LANES
    old, total = (n // group for n in own)
    old_other, total_other = (tiles + n // group for n in other)
    for t in [*range(old, total), *range(old_other, total_other)]:
        columns[span(t, t + 1), :] = jnp.broadcast_to(marks[0:1, span(t, t + 1)], (LANES, LANES)).T
    best = {t: state[:, span(t, t + 1)] for t in range(old)}
    best |= {t: jnp.full((8, LANES), -1.0, F32) for t in range(old, total)}

    def meet(left, right, first, stop):
        if first == stop:
            return
        step = max(2, 8 // (stop - first))
        for low in range(left, right, step):
            high = min(low + step, right)
            gram = lax.dot_general(
                keys[span(low, high), :],
                keys[span(first, stop), :],
                (((1,), (1,)), ((), ())),
                preferred_element_type=F32,
            )
            for key in range(low, high):
                column = columns[span(key, key + 1), :]
                for t in range(first, stop):
                    same = column == marks[0:1, span(t, t + 1)]
                    if t == key:
                        same = same & (iota((LANES, LANES), 0) != iota((LANES, LANES), 1))
                    piece = gram[span(key - low, key - low + 1), span(t - first, t - first + 1)]
                    piece = jnp.where(same, piece, -1.0)
                    top = jnp.max(piece.reshape(LANES // 8, 8, LANES), axis=0)
                    best[t] = jnp.maximum(best[t], top)

    def face(tile, left, right):
        across = jnp.full((LANES, LANES), -1.0, F32)
        column = columns[span(tile, tile + 1), :]
        for low in range(left, right, 8):
            high = min(low + 8, right)
            gram = lax.dot_general(
                keys[span(tile, tile + 1), :],
                keys[span(low, high), :],
                (((1,), (1,)), ((), ())),
                preferred_element_type=F32,
            )
            for t in range(low, high):
                same = column == marks[0:1, span(t, t + 1)]
                if t == tile:
                    same = same & (iota((LANES, LANES), 0) != iota((LANES, LANES), 1))
                piece = jnp.where(same, gram[:, span(t - low, t - low + 1)], -1.0)
                across = jnp.maximum(across, piece)
                if t < old:
                    top = jnp.max(piece.reshape(LANES // 8, 8, LANES), axis=0)
                    best[t] = jnp.maximum(best[t], top)
        top = jnp.max(across.T.reshape(LANES // 8, 8, LANES), axis=0)
        best[tile] = jnp.maximum(best[tile], top)

    if total - old == 1:
        face(old, 0, total)
        face(old, tiles, total_other)
    else:
        meet(0, total, old, total)
        meet(tiles, total_other, old, total)
        meet(old, total, 0, old)
    meet(old_other, total_other, 0, old)
    if total == tiles and old < tiles:
        count(marks, tiles, per_pair)
    if last is None:
        for t in range(total):
            state[:, span(t, t + 1)] = best[t]
    else:
        settle(best, marks, refs[4], capacity, last, per_pair)


def lay(values, first):
    total = jnp.sum(values, axis=1, keepdims=True)
    shape = (values.shape[0], LANES)
    return jnp.sum(jnp.where(iota(shape, 0) + first == iota(shape, 1), total, 0.0), axis=0, keepdims=True)


def labels_of(marks, tiles):
    return jnp.concatenate([marks[0:1, span(t, t + 1)] for t in range(tiles)], axis=0)


def count(marks, tiles, per_pair):
    mark = labels_of(marks, tiles)
    found = [jnp.sum((mark == k).astype(F32), axis=0, keepdims=True) for k in range(per_pair)]
    marks[1:2, 0:LANES] = lay(jnp.concatenate(found, axis=0), per_pair)


def settle(best, marks, out_ref, capacity, numbers, per_pair):
    pairs, tiles = len(numbers), len(best)
    owner = lax.axis_index("owner")
    chip, core = owner // 2, owner % 2
    rows = [jnp.max(best[t], axis=0, keepdims=True) for t in range(tiles)]
    row, mark = jnp.concatenate(rows, axis=0), labels_of(marks, tiles)
    sums = [jnp.sum(jnp.where(mark == k, row, 0.0), axis=0, keepdims=True) for k in range(per_pair)]
    stats = lay(jnp.concatenate(sums, axis=0), 0) + marks[1:2, 0:LANES]
    out_ref[:, span(1, 2)] = jnp.broadcast_to(stats, (2 * pairs, LANES))
    target = iota((2 * pairs, LANES), 0)
    back = jnp.zeros((2 * pairs, LANES), F32)
    for b, m in enumerate(numbers):
        line, shift = rows[b * capacity // LANES], b * capacity % LANES
        if shift:
            line = pltpu.roll(jnp.broadcast_to(line, (8, LANES)), LANES - shift, 1)[0:1, :]
        back = jnp.where(target == 2 * (chip ^ m) + core, line, back)
    out_ref[:, span(0, 1)] = back


def stage(new_own, new_other, own, other, state, items, width, capacity, per_pair, last):
    args = [near(b) for b in new_own + new_other]
    fresh = state is None
    out = [
        pltpu.VMEM((2 * items, width), BF16),
        pltpu.VMEM((8, 2 * items), F32),
        pltpu.VMEM((2 * items, LANES), F32),
        pltpu.VMEM((8, items), F32),
    ]
    aliases = {} if fresh else {len(args) + k: k for k in range(len(out))}
    args += [] if fresh else [near(a) for a in state]
    if last is not None:
        out.append(pltpu.VMEM((2 * len(last), 2 * LANES), F32))
    return pl.pallas_call(
        functools.partial(
            stage_kernel,
            own=own,
            other=other,
            fresh=fresh,
            items=items,
            capacity=capacity,
            per_pair=per_pair,
            last=last,
        ),
        in_specs=[VMEM] * len(args),
        out_specs=[VMEM] * len(out),
        out_shape=out,
        input_output_aliases=aliases,
        name="stage",
        compiler_params=PARAMS,
    )(*args)


def finish_kernel(back_ref, pair_ref, rank_ref, table_ref, maxima_ref, mean_ref, *, pairs, per_pair):
    core = lax.axis_index("owner") % 2
    pair, rank = pair_ref[...], rank_ref[...]
    maxima = jnp.zeros(pair.shape, F32)
    padded = table_ref.shape[1]
    pair_row, local_row = table_ref[0:1, :], table_ref[1:2, :]
    total = jnp.zeros((1, padded), F32)
    number = jnp.zeros((1, padded), F32)
    for p in range(pairs):
        got = jnp.where(core == 0, back_ref[2 * p : 2 * p + 1, span(0, 1)], back_ref[2 * p + 1 : 2 * p + 2, span(0, 1)])
        got = lane_take(got, rank)
        maxima = jnp.where(pair == p, got, maxima)
        stats = back_ref[2 * p : 2 * p + 1, span(1, 2)] + back_ref[2 * p + 1 : 2 * p + 2, span(1, 2)]
        mine = pair_row == p
        index = jnp.where(mine, local_row, 0)
        parts = [index[:, f : f + LANES] for f in range(0, padded, LANES)]
        sums = jnp.concatenate([lane_take(stats, i) for i in parts], axis=1)
        counts = jnp.concatenate([lane_take(stats, i + per_pair) for i in parts], axis=1)
        total = jnp.where(mine, sums, total)
        number = jnp.where(mine, counts, number)
    maxima_ref[...] = maxima
    mean = total / jnp.maximum(number, 1.0)
    mean_ref[...] = mean[:, : mean_ref.shape[1]]


def finish(back, pair, rank, table, clusters, pairs, per_pair):
    return pl.pallas_call(
        functools.partial(finish_kernel, pairs=pairs, per_pair=per_pair),
        in_specs=[VMEM] * 4,
        out_specs=[VMEM] * 2,
        out_shape=[
            jax.ShapeDtypeStruct(pair.shape, F32),
            jax.ShapeDtypeStruct((1, clusters), F32),
        ],
        name="finish",
        compiler_params=PARAMS,
    )(near(back), near(pair), near(rank), near(table))


def plan(pairs):
    size = pairs // 8
    part = [list(range(k * size, (k + 1) * size)) for k in range(8)]
    sent = part[6] + part[4] + part[5] + part[2] + part[7] + part[3] + part[1] + part[0]
    stages = [
        (part[0] + part[6] + part[2], part[0]),
        (part[3] + part[1], part[6] + part[2]),
        (part[4], part[3] + part[1]),
        (part[5], part[4]),
        ([], part[5]),
        (part[7], []),
        ([], part[7]),
    ]
    groups = [sent[:size], sent[size:]]
    return groups, stages


def body(embeddings, cluster_ids, owner_map):
    owners = lax.axis_size("owner")
    items, width = embeddings.shape
    clusters = owner_map.shape[0]
    pairs = owners // 2
    capacity = items // pairs
    per_pair = clusters // pairs
    ids = cluster_ids.reshape(items // LANES, LANES)
    groups, stages = plan(pairs)
    sent = [m for made in groups for m in made]
    *blocks, pair, rank, label, table, slot, rows = first_blocks(
        ids, owner_map.reshape(1, clusters), embeddings, groups[0], pairs, capacity
    )
    for made in groups[1:]:
        blocks += later_blocks(slot, label, rows, made, capacity)
    blocks = dict(zip(sent, blocks))
    swap = [(d, d ^ 1) for d in range(owners)]
    own, other = {}, {}
    for m in sent:
        own[m] = blocks[m]
        if m:
            own[m] = lax.ppermute(own[m], "owner", [(d, d ^ (2 * m)) for d in range(owners)])
    order = tuple(m for new, _ in stages for m in new)
    for m in order:
        other[m] = lax.ppermute(own[m], "owner", swap)
    state, mine, theirs = None, 0, 0
    for index, (new, swapped) in enumerate(stages):
        final = index == len(stages) - 1
        state = stage(
            [own[m] for m in new],
            [other[m] for m in swapped],
            (mine, mine + len(new)),
            (theirs, theirs + len(swapped)),
            state,
            items,
            width,
            capacity,
            per_pair,
            order if final else None,
        )
        mine, theirs = mine + len(new), theirs + len(swapped)
    back = lax.all_to_all(state[-1], "owner", split_axis=0, concat_axis=0, tiled=True)
    maxima, mean = finish(back, pair, rank, table, clusters, pairs, per_pair)
    return maxima.reshape(items), mean.reshape(clusters)


def solution(mesh):
    placed = (P(("parts", "owner"), None), P(("parts", "owner")), P("parts"))
    return jax.shard_map(
        body,
        mesh=mesh,
        in_specs=placed,
        out_specs=(P(("parts", "owner")), P("parts")),
        check_vma=False,
    )
```

```python
import functools

import jax
import jax.numpy as jnp
from jax import lax
from jax.experimental import pallas as pl
from jax.experimental.pallas import tpu as pltpu
from jax.sharding import PartitionSpec as P


LANES = 128
EXTRA = 8
CHUNKS = 4
F32 = jnp.float32
BF16 = jnp.bfloat16
VMEM = pl.BlockSpec(memory_space=pltpu.VMEM)
HBM = pl.BlockSpec(memory_space=pltpu.HBM)
PARAMS = pltpu.CompilerParams(vmem_limit_bytes=16 * 2**20)


def iota(shape, dim):
    return lax.broadcasted_iota(jnp.int32, shape, dim)


def near(value):
    return pltpu.with_memory_space_constraint(value, pltpu.VMEM)


def far(value):
    return pltpu.with_memory_space_constraint(value, pltpu.HBM)


def lane_take(row, index):
    if index.shape[0] == 1:
        return lane_take(row, jnp.broadcast_to(index, (8, LANES)))[0:1, :]
    out = None
    for first in range(0, row.shape[1], LANES):
        piece = jnp.broadcast_to(row[:, first : first + LANES], index.shape)
        local = index - first
        inside = (local >= 0) & (local < LANES)
        taken = jnp.take_along_axis(
            piece, jnp.where(inside, local, 0), axis=1, mode="promise_in_bounds"
        )
        out = taken if out is None else jnp.where(inside, taken, out)
    return out


def route(ids_ref, owners_ref, pair_ref, rank_ref, label_ref, table_ref, slot_ref, pad, pairs, clusters):
    chip = lax.axis_index("owner") // 2
    chunks = ids_ref.shape[0]
    padded = pad.shape[1]
    pad[...] = jnp.full(pad.shape, -2, jnp.int32)
    pad[0:1, 0:clusters] = owners_ref[...]
    pair_row = pad[0:1, :] >> 1
    across = jnp.broadcast_to(pair_row, (padded, padded))
    down = across.astype(F32).T.astype(jnp.int32)
    before = (across == down) & (iota(across.shape, 0) < iota(across.shape, 1))
    local_row = jnp.sum(before.astype(F32), axis=0, keepdims=True).astype(jnp.int32)
    table_ref[0:1, :] = pair_row
    table_ref[1:2, :] = local_row
    ids = ids_ref[...]
    pair = lane_take(pair_row, ids)
    label_ref[...] = lane_take(local_row, ids).astype(F32)
    hots = [pair == (chip ^ m) for m in range(pairs)]
    hot = jnp.concatenate([h.astype(F32) for h in hots], axis=0)
    upper = (iota((LANES, LANES), 0) <= iota((LANES, LANES), 1)).astype(BF16)
    within = jnp.dot(hot.astype(BF16), upper, preferred_element_type=F32)
    sums = jnp.dot(hot.astype(BF16), jnp.ones((LANES, LANES), BF16), preferred_element_type=F32)
    r, c = iota((pairs * chunks,) * 2, 0), iota((pairs * chunks,) * 2, 1)
    earlier = ((r // chunks == c // chunks) & (c < r)).astype(BF16)
    offset = jnp.dot(earlier, sums.astype(BF16), preferred_element_type=F32)
    slot = jnp.where(hot > 0.0, within + offset - 1.0, -1.0)
    item_rank = slot[0:chunks, :]
    for m in range(1, pairs):
        item_rank = jnp.maximum(item_rank, slot[m * chunks : (m + 1) * chunks, :])
    slot_ref[...] = slot
    pair_ref[...] = pair
    rank_ref[...] = item_rank.astype(jnp.int32)


def pack(slot_ref, label_ref, rows, blocks, numbers, capacity, arrived=None):
    chunks = label_ref.shape[0]
    width = rows.shape[1]
    slabs = width // LANES
    label = jnp.concatenate([label_ref[k : k + 1, :] for k in range(chunks)], axis=1)
    label = jnp.broadcast_to(label, (16, chunks * LANES)).astype(BF16)
    place = iota((capacity, LANES), 0).astype(F32)
    for block, m in zip(blocks, numbers):
        chosen = jnp.concatenate(
            [
                (place == slot_ref[m * chunks + k : m * chunks + k + 1, :]).astype(F32).astype(BF16)
                for k in range(chunks)
            ],
            axis=1,
        )
        if arrived is None:
            values = jnp.dot(chosen, rows[...], preferred_element_type=F32)
        else:
            values = jnp.zeros((capacity, width), F32)
            step = rows.shape[0] // len(arrived)
            for k, copy in enumerate(arrived):
                if block is blocks[0]:
                    copy.wait()
                piece = slice(k * step, (k + 1) * step)
                values += jnp.dot(chosen[:, piece], rows[piece, :], preferred_element_type=F32)
        scale = lax.rsqrt(jnp.mean(values * values, axis=1, keepdims=True) + 1e-06)
        unit = (values * scale * (1.0 / jnp.sqrt(F32(width)))).astype(BF16)
        labels = lax.dot_general(
            label, chosen, (((1,), (1,)), ((), ())), preferred_element_type=F32
        )
        for k in range(slabs):
            block[k * capacity : (k + 1) * capacity, :] = unit[:, k * LANES : (k + 1) * LANES]
        block[slabs * capacity : slabs * capacity + EXTRA, 0:capacity] = labels.astype(BF16)[0:EXTRA, :]


def first_kernel(ids_hbm, owners_hbm, rows_hbm, *refs, numbers, pairs, capacity, clusters):
    n = len(numbers)
    blocks = refs[:n]
    pair_ref, rank_ref, label_ref, table_ref, slot_ref, rows, ids_ref, owners_ref, pad, sems = refs[n:]
    step = rows.shape[0] // CHUNKS
    copies = [(ids_hbm, ids_ref), (owners_hbm, owners_ref)]
    for k in range(CHUNKS):
        piece = pl.ds(k * step, step)
        copies.append((rows_hbm.at[piece, :], rows.at[piece, :]))
    copies = [
        pltpu.make_async_copy(source, target, sems.at[k])
        for k, (source, target) in enumerate(copies)
    ]
    for copy in copies:
        copy.start()
    copies[0].wait()
    copies[1].wait()
    route(ids_ref, owners_ref, pair_ref, rank_ref, label_ref, table_ref, slot_ref, pad, pairs, clusters)
    pack(slot_ref, label_ref, rows, blocks, numbers, capacity, copies[2:])


def first_blocks(ids, owners, rows, numbers, pairs, capacity):
    clusters = owners.shape[1]
    padded = -(-clusters // LANES) * LANES
    height = rows.shape[1] // LANES * capacity + EXTRA
    return pl.pallas_call(
        functools.partial(
            first_kernel, numbers=numbers, pairs=pairs, capacity=capacity, clusters=clusters
        ),
        in_specs=[HBM] * 3,
        out_specs=[VMEM] * (len(numbers) + 6),
        out_shape=[pltpu.VMEM((height, LANES), BF16)] * len(numbers)
        + [
            pltpu.VMEM(ids.shape, jnp.int32),
            pltpu.VMEM(ids.shape, jnp.int32),
            pltpu.VMEM(ids.shape, F32),
            pltpu.VMEM((8, padded), jnp.int32),
            pltpu.VMEM((pairs * ids.shape[0], LANES), F32),
            pltpu.VMEM(rows.shape, BF16),
        ],
        scratch_shapes=[
            pltpu.VMEM(ids.shape, jnp.int32),
            pltpu.VMEM(owners.shape, jnp.int32),
            pltpu.VMEM((8, padded), jnp.int32),
            pltpu.SemaphoreType.DMA((2 + CHUNKS,)),
        ],
        name="first",
        compiler_params=PARAMS,
    )(far(ids), far(owners), far(rows))


def later_kernel(slot_ref, label_ref, rows_ref, *blocks, numbers, capacity):
    pack(slot_ref, label_ref, rows_ref, blocks, numbers, capacity)


def later_blocks(slot, label, rows, numbers, capacity):
    height = rows.shape[1] // LANES * capacity + EXTRA
    return pl.pallas_call(
        functools.partial(later_kernel, numbers=numbers, capacity=capacity),
        in_specs=[VMEM] * 3,
        out_specs=[VMEM] * len(numbers),
        out_shape=[pltpu.VMEM((height, LANES), BF16)] * len(numbers),
        name="later",
        compiler_params=PARAMS,
    )(near(slot), near(label), near(rows))


def span(first, stop):
    return slice(first * LANES, stop * LANES)


def place(block, keys, marks, at, capacity):
    slabs = keys.shape[1] // LANES
    for k in range(slabs):
        keys[at : at + capacity, k * LANES : (k + 1) * LANES] = block[
            k * capacity : (k + 1) * capacity, :
        ]
    marks[0:1, at : at + capacity] = block[
        slabs * capacity : slabs * capacity + EXTRA, 0:capacity
    ].astype(F32)[0:1, :]


def stage_kernel(*refs, own, other, fresh, items, capacity, per_pair, last):
    refs = list(refs)
    blocks = [refs.pop(0) for _ in range(own[1] - own[0] + other[1] - other[0])]
    if not fresh:
        refs = refs[4:]
    keys, marks, columns, state = refs[:4]
    starts = [b * capacity for b in range(*own)] + [items + b * capacity for b in range(*other)]
    for block, at in zip(blocks, starts):
        place(block, keys, marks, at, capacity)
    group, tiles = LANES // capacity, items // LANES
    old, total = (n // group for n in own)
    old_other, total_other = (tiles + n // group for n in other)
    for t in [*range(old, total), *range(old_other, total_other)]:
        columns[span(t, t + 1), :] = jnp.broadcast_to(marks[0:1, span(t, t + 1)], (LANES, LANES)).T
    best = {t: state[:, span(t, t + 1)] for t in range(old)}
    best |= {t: jnp.full((8, LANES), -1.0, F32) for t in range(old, total)}

    def meet(left, right, first, stop):
        if first == stop:
            return
        step = max(2, 8 // (stop - first))
        for low in range(left, right, step):
            high = min(low + step, right)
            gram = lax.dot_general(
                keys[span(low, high), :],
                keys[span(first, stop), :],
                (((1,), (1,)), ((), ())),
                preferred_element_type=F32,
            )
            for key in range(low, high):
                column = columns[span(key, key + 1), :]
                for t in range(first, stop):
                    same = column == marks[0:1, span(t, t + 1)]
                    if t == key:
                        same = same & (iota((LANES, LANES), 0) != iota((LANES, LANES), 1))
                    piece = gram[span(key - low, key - low + 1), span(t - first, t - first + 1)]
                    piece = jnp.where(same, piece, -1.0)
                    top = jnp.max(piece.reshape(LANES // 8, 8, LANES), axis=0)
                    best[t] = jnp.maximum(best[t], top)

    def face(tile, left, right):
        across = jnp.full((LANES, LANES), -1.0, F32)
        column = columns[span(tile, tile + 1), :]
        for low in range(left, right, 8):
            high = min(low + 8, right)
            gram = lax.dot_general(
                keys[span(tile, tile + 1), :],
                keys[span(low, high), :],
                (((1,), (1,)), ((), ())),
                preferred_element_type=F32,
            )
            for t in range(low, high):
                same = column == marks[0:1, span(t, t + 1)]
                if t == tile:
                    same = same & (iota((LANES, LANES), 0) != iota((LANES, LANES), 1))
                piece = jnp.where(same, gram[:, span(t - low, t - low + 1)], -1.0)
                across = jnp.maximum(across, piece)
                if t < old:
                    top = jnp.max(piece.reshape(LANES // 8, 8, LANES), axis=0)
                    best[t] = jnp.maximum(best[t], top)
        top = jnp.max(across.T.reshape(LANES // 8, 8, LANES), axis=0)
        best[tile] = jnp.maximum(best[tile], top)

    if total - old == 1:
        face(old, 0, total)
        face(old, tiles, total_other)
    else:
        meet(0, total, old, total)
        meet(tiles, total_other, old, total)
        meet(old, total, 0, old)
    meet(old_other, total_other, 0, old)
    if total == tiles and old < tiles:
        count(marks, tiles, per_pair)
    if last is None:
        for t in range(total):
            state[:, span(t, t + 1)] = best[t]
    else:
        settle(best, marks, refs[4], capacity, last, per_pair)


def lay(values, first):
    total = jnp.sum(values, axis=1, keepdims=True)
    shape = (values.shape[0], LANES)
    return jnp.sum(jnp.where(iota(shape, 0) + first == iota(shape, 1), total, 0.0), axis=0, keepdims=True)


def labels_of(marks, tiles):
    return jnp.concatenate([marks[0:1, span(t, t + 1)] for t in range(tiles)], axis=0)


def count(marks, tiles, per_pair):
    mark = labels_of(marks, tiles)
    found = [jnp.sum((mark == k).astype(F32), axis=0, keepdims=True) for k in range(per_pair)]
    marks[1:2, 0:LANES] = lay(jnp.concatenate(found, axis=0), per_pair)


def settle(best, marks, out_ref, capacity, numbers, per_pair):
    pairs, tiles = len(numbers), len(best)
    owner = lax.axis_index("owner")
    chip, core = owner // 2, owner % 2
    rows = [jnp.max(best[t], axis=0, keepdims=True) for t in range(tiles)]
    row, mark = jnp.concatenate(rows, axis=0), labels_of(marks, tiles)
    sums = [jnp.sum(jnp.where(mark == k, row, 0.0), axis=0, keepdims=True) for k in range(per_pair)]
    stats = lay(jnp.concatenate(sums, axis=0), 0) + marks[1:2, 0:LANES]
    out_ref[:, span(1, 2)] = jnp.broadcast_to(stats, (2 * pairs, LANES))
    target = iota((2 * pairs, LANES), 0)
    back = jnp.zeros((2 * pairs, LANES), F32)
    for b, m in enumerate(numbers):
        line, shift = rows[b * capacity // LANES], b * capacity % LANES
        if shift:
            line = pltpu.roll(jnp.broadcast_to(line, (8, LANES)), LANES - shift, 1)[0:1, :]
        back = jnp.where(target == 2 * (chip ^ m) + core, line, back)
    out_ref[:, span(0, 1)] = back


def stage(new_own, new_other, own, other, state, items, width, capacity, per_pair, last):
    args = [near(b) for b in new_own + new_other]
    fresh = state is None
    out = [
        pltpu.VMEM((2 * items, width), BF16),
        pltpu.VMEM((8, 2 * items), F32),
        pltpu.VMEM((2 * items, LANES), F32),
        pltpu.VMEM((8, items), F32),
    ]
    aliases = {} if fresh else {len(args) + k: k for k in range(len(out))}
    args += [] if fresh else [near(a) for a in state]
    if last is not None:
        out.append(pltpu.VMEM((2 * len(last), 2 * LANES), F32))
    return pl.pallas_call(
        functools.partial(
            stage_kernel,
            own=own,
            other=other,
            fresh=fresh,
            items=items,
            capacity=capacity,
            per_pair=per_pair,
            last=last,
        ),
        in_specs=[VMEM] * len(args),
        out_specs=[VMEM] * len(out),
        out_shape=out,
        input_output_aliases=aliases,
        name="stage",
        compiler_params=PARAMS,
    )(*args)


def finish_kernel(back_ref, pair_ref, rank_ref, table_ref, maxima_ref, mean_ref, *, pairs, per_pair):
    core = lax.axis_index("owner") % 2
    pair, rank = pair_ref[...], rank_ref[...]
    maxima = jnp.zeros(pair.shape, F32)
    padded = table_ref.shape[1]
    pair_row, local_row = table_ref[0:1, :], table_ref[1:2, :]
    total = jnp.zeros((1, padded), F32)
    number = jnp.zeros((1, padded), F32)
    for p in range(pairs):
        got = jnp.where(core == 0, back_ref[2 * p : 2 * p + 1, span(0, 1)], back_ref[2 * p + 1 : 2 * p + 2, span(0, 1)])
        got = lane_take(got, rank)
        maxima = jnp.where(pair == p, got, maxima)
        stats = back_ref[2 * p : 2 * p + 1, span(1, 2)] + back_ref[2 * p + 1 : 2 * p + 2, span(1, 2)]
        mine = pair_row == p
        index = jnp.where(mine, local_row, 0)
        parts = [index[:, f : f + LANES] for f in range(0, padded, LANES)]
        sums = jnp.concatenate([lane_take(stats, i) for i in parts], axis=1)
        counts = jnp.concatenate([lane_take(stats, i + per_pair) for i in parts], axis=1)
        total = jnp.where(mine, sums, total)
        number = jnp.where(mine, counts, number)
    maxima_ref[...] = maxima
    mean = total / jnp.maximum(number, 1.0)
    mean_ref[...] = mean[:, : mean_ref.shape[1]]


def finish(back, pair, rank, table, clusters, pairs, per_pair):
    return pl.pallas_call(
        functools.partial(finish_kernel, pairs=pairs, per_pair=per_pair),
        in_specs=[VMEM] * 4,
        out_specs=[VMEM] * 2,
        out_shape=[
            jax.ShapeDtypeStruct(pair.shape, F32),
            jax.ShapeDtypeStruct((1, clusters), F32),
        ],
        name="finish",
        compiler_params=PARAMS,
    )(near(back), near(pair), near(rank), near(table))


def plan(pairs):
    size = pairs // 8
    part = [list(range(k * size, (k + 1) * size)) for k in range(8)]
    sent = part[6] + part[4] + part[5] + part[2] + part[7] + part[1] + part[3] + part[0]
    stages = [
        (part[0] + part[6] + part[2], part[0]),
        (part[3] + part[1], part[6] + part[2]),
        (part[4], part[3] + part[1]),
        (part[5], part[4]),
        (part[7], []),
        ([], part[5] + part[7]),
    ]
    groups = [sent[:size], sent[size:]]
    return groups, stages


def body(embeddings, cluster_ids, owner_map):
    owners = lax.axis_size("owner")
    items, width = embeddings.shape
    clusters = owner_map.shape[0]
    pairs = owners // 2
    capacity = items // pairs
    per_pair = clusters // pairs
    ids = cluster_ids.reshape(items // LANES, LANES)
    groups, stages = plan(pairs)
    sent = [m for made in groups for m in made]
    *blocks, pair, rank, label, table, slot, rows = first_blocks(
        ids, owner_map.reshape(1, clusters), embeddings, groups[0], pairs, capacity
    )
    for made in groups[1:]:
        blocks += later_blocks(slot, label, rows, made, capacity)
    blocks = dict(zip(sent, blocks))
    swap = [(d, d ^ 1) for d in range(owners)]
    own, other = {}, {}
    for m in sent:
        own[m] = blocks[m]
        if m:
            own[m] = lax.ppermute(own[m], "owner", [(d, d ^ (2 * m)) for d in range(owners)])
    order = tuple(m for new, _ in stages for m in new)
    for m in order:
        other[m] = lax.ppermute(own[m], "owner", swap)
    state, mine, theirs = None, 0, 0
    for index, (new, swapped) in enumerate(stages):
        final = index == len(stages) - 1
        state = stage(
            [own[m] for m in new],
            [other[m] for m in swapped],
            (mine, mine + len(new)),
            (theirs, theirs + len(swapped)),
            state,
            items,
            width,
            capacity,
            per_pair,
            order if final else None,
        )
        mine, theirs = mine + len(new), theirs + len(swapped)
    back = lax.all_to_all(state[-1], "owner", split_axis=0, concat_axis=0, tiled=True)
    maxima, mean = finish(back, pair, rank, table, clusters, pairs, per_pair)
    return maxima.reshape(items), mean.reshape(clusters)


def solution(mesh):
    placed = (P(("parts", "owner"), None), P(("parts", "owner")), P("parts"))
    return jax.shard_map(
        body,
        mesh=mesh,
        in_specs=placed,
        out_specs=(P(("parts", "owner")), P("parts")),
        check_vma=False,
    )
```
